128 devices in a mesh: band: 4 (over y), fft: 32 (over z, x, core).
Axes of the slice: x: 4, y: 4, z: 4, core: 2. Of those that a mesh axis runs over, the one named last changes fastest.
Arguments:
- new_bands: bfloat16 [2, 8, 2048, 192], P(None, None, ('band', 'fft')), may hold values from -6 to 6
- resident: bfloat16 [2, 128, 2048, 192], P(None, None, ('band', 'fft')), may hold values from -0.009765625 to 0.009765625
- potential: float32 [192, 192, 192], P('fft'), may hold values from 0.5 to 2.5
- stick_pos: int32 [2048], replicated, may hold values from 0 to 36863, as said below
- stick_count: int32 [128], P(('band', 'fft')), may hold values from 1 to 16, 1024 in all
Outputs:
- applied: bfloat16 [2, 8, 2048, 192], P(None, None, ('band', 'fft'))
- projection: float32 [2, 128, 8], replicated
- intersection: float32 [2, 128, 8], replicated
The draws below stay inside these ranges and needn't reach their ends.
Inputs may be any that keep to these rules, and one draw needn't show every extreme that they name: The first stick_count[d] slots of device d (slots d * 16 onward) hold live sticks and the rest are padding; the counts sum to 1024. `stick_pos`: all slots name distinct columns; every column's x is below 48 or at least 144.
All inputs are finite; a program needn't handle non-finite values.
Results may differ from the reference program's by a relative error of at most 0.001.
Values sent between devices are 32-bit elements; how exact they have to be, the bound alone decides.
No kernel may reach another device: no remote copies, remote signals or barrier semaphores. Data moves between devices by JAX's collectives and lax.ppermute only.
A program may use at most 128 MiB of HBM per device.

```python
import math
import jax
import jax.numpy as jnp
import numpy as np
from jax import lax

NBOX = 192
RES = 128
SLOTS_DEV = 16
NEW = 8
SLOTS = 2048
LIVE = 1024
N_BAND = 4
N_FFT = 32


def draw_stick_pos(key, part):
    allowed = NBOX * NBOX // 2
    middle = jax.random.permutation(jax.random.fold_in(key, 11), allowed - 2)[:SLOTS - 2] + 1
    chosen = jnp.concatenate([jnp.array([0, allowed - 1], jnp.int32), middle.astype(jnp.int32)])
    shuffle = jax.random.permutation(jax.random.fold_in(key, 12), SLOTS)
    chosen = chosen[shuffle]
    box_row = chosen // NBOX
    box_column = chosen % NBOX
    grid_row = jnp.where(box_row < NBOX // 4, box_row, box_row + NBOX // 2)
    return (grid_row * NBOX + box_column).astype(jnp.int32)


def block_levels(stream_key, extent, shards, smallest, top_value):
    level = 1.0
    for dim, parts in shards:
        draws = jax.random.uniform(jax.random.fold_in(jax.random.fold_in(stream_key, 6), dim), (parts,), jnp.float32, smallest / len(shards), top_value / len(shards))
        level = level * jnp.repeat(jnp.exp(draws), extent[dim] // parts).reshape((-1,) + (1,) * (len(extent) - 1 - dim))
    return level


def profile(amount, total, most, lean):
    portions = [(1 << 20) // math.isqrt(grade ** lean) + 1 for grade in range(2, amount + 1)]
    spare, given = total - most - (amount - 1), [1] * (amount - 1)
    while spare > 0:
        candidates = [i for i in range(amount - 1) if given[i] < most]
        whole, left = sum([portions[i] for i in candidates]), spare
        for i in candidates:
            addition = min(most - given[i], max(1, left * portions[i] // whole), spare)
            given[i] = given[i] + addition
            spare = spare - addition
    return np.array([most] + given)


def ragged_sizes(own_key, amount, total, limit, slope):
    if amount == 2:
        one = jax.random.randint(own_key, (), max(1, total - limit), min(limit, total - 1) + 1)
        return jnp.stack([one, total - one])
    lengths = jnp.asarray(profile(amount, total, limit, slope), jnp.int32)
    pairs = (amount - 1) // 2
    giver, sink = lengths[1:1 + 2 * pairs:2], lengths[2:2 + 2 * pairs:2]
    margin = jnp.minimum(giver - 1, limit - sink)
    passed = jax.random.randint(jax.random.fold_in(own_key, 1), (pairs,), 0, 1 << 20) % (margin + 1)
    lengths = lengths.at[1:1 + 2 * pairs:2].set(giver - passed).at[2:2 + 2 * pairs:2].set(sink + passed)
    return lengths[jax.random.permutation(jax.random.fold_in(own_key, 2), amount)]


def centred(own_key, extent, deviation, limit, shards=(), held_as=jnp.bfloat16):
    values = deviation * jax.random.normal(own_key, extent, jnp.float32)
    if shards:
        values = values * block_levels(own_key, extent, shards, -0.22, 0.18)
    return jnp.clip(values, -limit, limit).astype(held_as)


def setup_inputs(seed: int = 0) -> dict:
    streams_of = jax.random.split(jax.random.key(seed), 6)
    new_bands = centred(streams_of[0], (2, NEW, SLOTS, NBOX), 1.0, 6.0, ((2, 128),))
    resident = centred(streams_of[1], (2, RES, SLOTS, NBOX), (2 * LIVE * NBOX) ** -0.5, 0.009765625, ((2, 128),))
    potential = jnp.clip(0.5 + 2.0 * jax.random.uniform(streams_of[2], (NBOX, NBOX, NBOX), jnp.float32) ** block_levels(streams_of[2], (NBOX, NBOX, NBOX), ((0, 32),), -0.2, 0.2), 0.5, 2.5)
    stick_pos = draw_stick_pos(jax.random.fold_in(streams_of[5], 71), 0)
    stick_count = ragged_sizes(streams_of[4], N_BAND * N_FFT, LIVE, SLOTS_DEV, 2).astype(jnp.int32)
    return dict(new_bands=new_bands, resident=resident, potential=potential, stick_pos=stick_pos, stick_count=stick_count)


kinetic_scale = 2.0


def folded(values, length):
    return jnp.where(values < length // 2, values, values - length).astype(jnp.float32)


def kinetic_table(positions, length):
    grid_x = positions // length
    grid_y = positions % length
    freq_z = folded(jnp.arange(length, dtype=jnp.int32), length)
    squares = folded(grid_x, length) ** 2 + folded(grid_y, length) ** 2
    return kinetic_scale * (squares[:, None] + freq_z[None, :] ** 2) / (length * length)


def swapped(vectors):
    return jnp.stack([vectors[1], -vectors[0]])


def reference(new_bands, resident, potential, stick_pos, stick_count):
    slot_ids = jnp.arange(SLOTS, dtype=jnp.int32)
    slot_live = ((slot_ids % SLOTS_DEV) < stick_count[slot_ids // SLOTS_DEV]).astype(jnp.float32)
    live_bands = new_bands * slot_live.astype(jnp.bfloat16)[None, None, :, None]
    coeffs = live_bands.astype(jnp.float32)
    kinetic = kinetic_table(stick_pos, NBOX)
    potential_xyz = jnp.transpose(potential, (1, 2, 0))

    def one_band(band_coeffs):
        freq_box = jnp.zeros((2, NBOX * NBOX, NBOX), jnp.float32).at[:, stick_pos, :].set(band_coeffs)
        freq_box = freq_box.reshape(2, NBOX, NBOX, NBOX)
        real_field = jnp.fft.ifftn(lax.complex(freq_box[0], freq_box[1])) * (NBOX ** 3)
        spectrum = jnp.fft.fftn(real_field * potential_xyz) / (NBOX ** 3)
        spectrum = spectrum.reshape(NBOX * NBOX, NBOX)[stick_pos]
        return jnp.stack([jnp.real(spectrum), jnp.imag(spectrum)])

    spectra = lax.map(one_band, jnp.transpose(coeffs, (1, 0, 2, 3)))
    spectra = jnp.transpose(spectra, (1, 0, 2, 3))
    applied = ((kinetic[None, None] * coeffs + spectra) * slot_live[None, None, :, None]).astype(jnp.bfloat16)
    operands = jnp.stack([applied, swapped(applied), live_bands, swapped(live_bands)])
    totals = jnp.zeros((RES, 4 * NEW), jnp.float32)
    for component in range(2):
        left = resident[component].reshape(RES, SLOTS * NBOX).astype(jnp.float32)
        right = operands[:, component].reshape(4 * NEW, SLOTS * NBOX).astype(jnp.float32)
        totals = totals + jnp.dot(left, right.T, preferred_element_type=jnp.float32)
    totals = totals.reshape(RES, 4, NEW)
    projection = jnp.stack([totals[:, 0], totals[:, 1]])
    intersection = jnp.stack([totals[:, 2], totals[:, 3]])
    return applied, projection, intersection
```

```python
import functools

import jax
import jax.numpy as jnp
import ml_dtypes
import numpy as np
from jax import lax
from jax.experimental import pallas as pl
from jax.experimental.pallas import tpu as pltpu
from jax.sharding import PartitionSpec as P

BOX = 192
HALF = 96
SLOTS_DEV = 16
NEW = 8
RES = 128
DEVICES = 128
PLANES = 6
GROUPS = 4
COLUMNS = 32
ROWS_X = 96
f32 = jnp.float32
bf16 = jnp.bfloat16
both = ("band", "fft")


def halves(table):
    high = table.astype(ml_dtypes.bfloat16)
    low = (table - high.astype(np.float64)).astype(ml_dtypes.bfloat16)
    return high, low


def wave(rows, cols):
    return 2.0 * np.pi / BOX * ((rows[:, None] * cols[None, :]) % BOX)


def rotation(angles):
    return [[np.cos(angles), -np.sin(angles)], [np.sin(angles), np.cos(angles)]]


def make_tables():
    plane = (np.arange(COLUMNS)[None, :] * PLANES + np.arange(PLANES)[:, None]).reshape(-1)
    blocks = rotation(wave(plane, np.arange(BOX)))
    z_table = []
    for q in range(2):
        high, low = halves(np.concatenate([blocks[0][q], blocks[1][q]], axis=0))
        z_table.append(np.concatenate([high, low], axis=0))
    z_table = np.stack(z_table)
    y_table = []
    for odd in range(2):
        blocks = rotation(wave(2 * np.arange(HALF) + odd, np.arange(HALF)))
        full = np.zeros((2, 128, 2, 128))
        for q_in in range(2):
            for q_out in range(2):
                full[q_in, :HALF, q_out, :HALF] = blocks[q_out][q_in]
        y_table.append(np.stack(halves(full.reshape(256, 256))))
    y_table = np.stack(y_table)
    index = np.concatenate([2 * np.arange(48), 2 * np.arange(48) + 1])
    freq = np.where(index < 48, index, index + 96)
    blocks = rotation(wave(np.arange(BOX), freq))
    to_x = np.block(blocks)
    to_x = np.stack(halves(to_x))
    from_x = []
    for odd in range(2):
        angles = -wave(freq[odd * 48 : odd * 48 + 48], np.arange(HALF))
        from_x.append(np.stack(halves(np.block(rotation(angles)))))
    return z_table, y_table, to_x, np.stack(from_x)


def dot(a, b):
    return lax.dot_general(a, b, (((1,), (0,)), ((), ())), preferred_element_type=f32)


def dot_nt(a, b):
    return lax.dot_general(a, b, (((1,), (1,)), ((), ())), preferred_element_type=f32)


def split(values):
    high = values.astype(bf16)
    return high, (values - high.astype(f32)).astype(bf16)


def stick_sums(res_ref, parts, halves_ref):
    for q in range(2):
        halves_ref[q, 0] = parts[q][:, :128].astype(f32)
        halves_ref[q, 1, :, 0:64] = parts[q][:, 128:].astype(f32)
    total = jnp.zeros((16, 128), f32)
    for slot in range(SLOTS_DEV):
        for half, width in ((0, 128), (1, 64)):
            v0 = halves_ref[0, half, pl.ds(slot, 8, stride=16), :][:, :width]
            v1 = halves_ref[1, half, pl.ds(slot, 8, stride=16), :][:, :width]
            rows = slice(half * 128, half * 128 + width)
            total = total + dot(jnp.concatenate([v0, v1], axis=0).astype(bf16), res_ref[0, slot, rows, :])
            total = total + dot(jnp.concatenate([v1, -v0], axis=0).astype(bf16), res_ref[1, slot, rows, :])
    return total


def live_parts(count, nb_ref):
    row = lax.broadcasted_iota(jnp.int32, (NEW * SLOTS_DEV, BOX), 0) & (SLOTS_DEV - 1)
    live = row < count
    return [
        jnp.where(live, nb_ref[q].reshape(NEW * SLOTS_DEV, BOX).astype(f32), 0.0).astype(bf16)
        for q in range(2)
    ]


def send_kernel(count_ref, nb_ref, res_ref, z_ref, out_ref, halves_ref):
    parts = live_parts(count_ref[0], nb_ref)
    acc = dot_nt(z_ref[0], parts[0]) + dot_nt(z_ref[1], parts[1])
    acc = acc[:384] + acc[384:]
    lane = lax.broadcasted_iota(jnp.int32, (COLUMNS, 128), 1) // 32
    for k in range(3):
        for group in range(GROUPS):
            total = jnp.zeros((COLUMNS, 128), f32)
            for c in range(4):
                piece = acc[(k * 4 + c) * 32 : (k * 4 + c + 1) * 32]
                shift = (c - group) * 32 % 128
                if shift:
                    piece = pltpu.roll(piece, shift, 1)
                total = jnp.where(lane == c, piece, total)
            out_ref[pl.ds(group * 128 + k, 32, stride=4), :] = total
    out_ref[pl.ds(3, 16, stride=4), :] = stick_sums(res_ref, parts, halves_ref)
    out_ref[pl.ds(67, 112, stride=4), :] = jnp.zeros((112, 128), f32)


def place_kernel(pos_ref, pot_ref, pick_ref, mask_ref, wide_ref, pad_ref):
    pos = pos_ref[...].astype(f32)
    row = jnp.floor((pos + 0.5) * (1.0 / BOX))
    col = pos - row * BOX
    half = jnp.floor(col * 0.5)
    lane_of = half + (col - 2.0 * half) * 128.0
    row = jnp.where(row < 48.0, row, row - 96.0)
    half = jnp.floor(row * 0.5)
    row = jnp.transpose(half + (row - 2.0 * half) * 48.0)
    lane = lax.broadcasted_iota(jnp.int32, (DEVICES, 256), 1).astype(f32)
    index = lax.broadcasted_iota(jnp.int32, (ROWS_X, 128), 0).astype(f32)
    for slot in range(SLOTS_DEV):
        hit = lane_of[:, slot : slot + 1] == lane
        pick_ref[slot * 128 : (slot + 1) * 128, :] = jnp.where(hit, 1.0, 0.0).astype(bf16)
        hit = jnp.where(jnp.broadcast_to(row[slot : slot + 1, :], (ROWS_X, 128)) == index, 1.0, 0.0)
        mask_ref[:, slot * 128 : (slot + 1) * 128] = hit.astype(bf16)
        wide_ref[:, slot * 128 : (slot + 1) * 128] = hit
    gap = jnp.zeros((BOX, 32), f32)
    for p in range(PLANES):
        value = pot_ref[p]
        pad_ref[p] = jnp.concatenate([value[:, :HALF], gap, value[:, HALF:], gap], axis=1)


CHUNK = 4


def box_kernel(
    in_ref, pot_any, pick_any, mask_any, wide_any, y_any, tox_any, fromx_any, out_ref,
    flat, high_v, low_v, grid, mid_h, mid_l, back, picked,
    pot_ref, pick_ref, mask_ref, wide_ref, y_ref, tox_ref, fromx_ref, sems,
):
    moves = [
        pltpu.make_async_copy(source, target, sems.at[i])
        for i, (source, target) in enumerate((
            (mask_any, mask_ref), (pick_any, pick_ref), (y_any, y_ref), (tox_any, tox_ref),
            (pot_any, pot_ref), (fromx_any, fromx_ref), (wide_any, wide_ref),
        ))
    ]
    for move in moves:
        move.start()
    for k in range(3):
        flat[k * 128 : (k + 1) * 128, :] = jnp.transpose(in_ref[pl.ds(k, 128, stride=4), :])
    for slot in range(SLOTS_DEV):
        lanes = slice(slot * 128, (slot + 1) * 128)
        values = flat[pl.ds(slot, 24, stride=16), :]
        high = values.astype(bf16).astype(f32)
        high_v[:, lanes] = high
        low_v[:, lanes] = values - high

    def scatter(chunk, carry):
        sums = None
        for source in (high_v, low_v):
            blocks = []
            for i in range(CHUNK):
                value = source[pl.ds(chunk * CHUNK + i, 1), :]
                value = jnp.broadcast_to(value, (16, 2048)).astype(bf16)
                blocks.append(mask_ref[...] * jnp.concatenate([value] * 6, axis=0))
            term = dot(jnp.concatenate(blocks, axis=0), pick_ref[...])
            sums = term if sums is None else sums + term
        start = pl.multiple_of(chunk * (CHUNK * 96), 8)
        for odd in range(2):
            grid[odd, pl.ds(start, CHUNK * 96), :] = sums[:, odd * 128 : odd * 128 + 128]
        return carry

    for move in moves[:2]:
        move.wait()
    lax.fori_loop(0, 24 // CHUNK, scatter, 0)
    for move in moves[2:]:
        move.wait()

    for part in range(2):
        outs = []
        for odd in range(2):
            re = grid[odd, part * 576 : part * 576 + 576, :]
            im = grid[odd, 1152 + part * 576 : 1152 + part * 576 + 576, :]
            high, low = split(jnp.concatenate([re, im], axis=1))
            outs.append(dot(high, y_ref[odd, 0]) + dot(low, y_ref[odd, 0]) + dot(high, y_ref[odd, 1]))
        plus, minus = outs[0] + outs[1], outs[0] - outs[1]
        for q in range(2):
            lanes = slice(q * 128, q * 128 + 128)
            high, low = split(jnp.concatenate([plus[:, lanes], minus[:, lanes]], axis=1))
            for i in range(6):
                mid_h[part * 6 + i, q * 96 : q * 96 + 96, :] = high[i * 96 : i * 96 + 96]
                mid_l[part * 6 + i, q * 96 : q * 96 + 96, :] = low[i * 96 : i * 96 + 96]

    def one_plane(i, weight):
        high, low = mid_h[i], mid_l[i]
        field = dot(tox_ref[0], high) + dot(tox_ref[1], high) + dot(tox_ref[0], low)
        re, im = field[:192] * weight, field[192:] * weight
        for odd in range(2):
            if odd:
                folded = jnp.concatenate([re[:96] - re[96:], im[:96] - im[96:]], axis=0)
            else:
                folded = jnp.concatenate([re[:96] + re[96:], im[:96] + im[96:]], axis=0)
            high, low = split(folded)
            out = dot(fromx_ref[odd, 0], high) + dot(fromx_ref[odd, 1], high) + dot(fromx_ref[odd, 0], low)
            start = pl.multiple_of(i * 96 + odd * 48, 8)
            back[pl.ds(start, 48), :] = out[:48]
            back[pl.ds(start + 1152, 48), :] = out[48:]

    def plane(p, carry):
        weight = pot_ref[p]
        for i in range(2):
            one_plane(2 * p + i, weight)
        return carry

    lax.fori_loop(0, PLANES, plane, 0)

    for part in range(2):
        re = back[part * 576 : part * 576 + 576, :]
        im = back[1152 + part * 576 : 1152 + part * 576 + 576, :]
        outs = []
        for odd in range(2):
            if odd:
                pair = [re[:, :128] - re[:, 128:], im[:, :128] - im[:, 128:]]
            else:
                pair = [re[:, :128] + re[:, 128:], im[:, :128] + im[:, 128:]]
            high, low = split(jnp.concatenate(pair, axis=1))
            outs.append(
                dot_nt(high, y_ref[odd, 0]) + dot_nt(low, y_ref[odd, 0]) + dot_nt(high, y_ref[odd, 1])
            )
        for q in range(2):
            lanes = slice(q * 128, q * 128 + 128)
            start = q * 1152 + part * 576
            for odd in range(2):
                high, low = split(outs[odd][:, lanes])
                picked[start : start + 576, odd * 128 : odd * 128 + 128] = high
                picked[start : start + 576, odd * 128 + 256 : odd * 128 + 384] = low

    def pick(tile, carry):
        start = pl.multiple_of(tile * 256, 256)
        sel = pick_ref[pl.ds(start, 256), :]
        out = dot_nt(picked[...], jnp.concatenate([sel, sel], axis=1))
        mask = wide_ref[:, pl.ds(start, 256)]
        total = jnp.sum(out.reshape(24, ROWS_X, 256) * mask[None], axis=1)
        flat[pl.ds(2 * tile, 24, stride=16), :] = total[:, :128]
        flat[pl.ds(2 * tile + 1, 24, stride=16), :] = total[:, 128:]
        return carry

    lax.fori_loop(0, 8, pick, 0)

    for k in range(3):
        out_ref[pl.ds(k, 128, stride=4), :] = jnp.transpose(flat[k * 128 : (k + 1) * 128, :])
    total = jnp.sum(in_ref[pl.ds(3, 128, stride=4), :], axis=0, keepdims=True)
    out_ref[pl.ds(3, 128, stride=4), :] = jnp.broadcast_to(total, (DEVICES, 128))


def apply_kernel(
    count_ref, pos_ref, in_ref, nb_ref, res_ref, z_ref, applied_ref, keep_ref, give_ref, inter_ref,
    halves_ref,
):
    device = lax.axis_index("band") * COLUMNS + lax.axis_index("fft")
    lane = lax.broadcasted_iota(jnp.int32, (COLUMNS, 128), 1) // 32
    pieces = []
    for k in range(3):
        for c in range(4):
            total = jnp.zeros((COLUMNS, 128), f32)
            for group in range(GROUPS):
                piece = in_ref[pl.ds(group * 128 + k, 32, stride=4), :]
                shift = (group - c) * 32 % 128
                if shift:
                    piece = pltpu.roll(piece, shift, 1)
                total = jnp.where(lane == group, piece, total)
            pieces.append(total)
    field = jnp.transpose(jnp.concatenate(pieces, axis=0))
    high, low = split(field)
    parts = live_parts(count_ref[0], nb_ref)
    row = lax.broadcasted_iota(jnp.int32, (NEW * SLOTS_DEV, BOX), 0) & (SLOTS_DEV - 1)
    squares = jnp.zeros((NEW * SLOTS_DEV, BOX), f32)
    for slot in range(SLOTS_DEV):
        pos = pos_ref[device * SLOTS_DEV + slot]
        kx = lax.div(pos, jnp.int32(BOX))
        ky = pos - kx * BOX
        kx = jnp.where(kx < HALF, kx, kx - BOX)
        ky = jnp.where(ky < HALF, ky, ky - BOX)
        squares = jnp.where(row == slot, (kx * kx + ky * ky).astype(f32), squares)
    kz = lax.broadcasted_iota(jnp.int32, (NEW * SLOTS_DEV, BOX), 1)
    kz = jnp.where(kz < HALF, kz, kz - BOX).astype(f32)
    kinetic = 2.0 * (squares + kz * kz) / float(BOX * BOX)
    live = row < count_ref[0]
    applied = []
    for q in range(2):
        table = z_ref[q]
        spectrum = dot(high, table[:384]) + dot(low, table[:384]) + dot(high, table[384:])
        spectrum = spectrum * (1.0 / BOX**3)
        value = jnp.where(live, kinetic * parts[q].astype(f32) + spectrum, 0.0).astype(bf16)
        applied.append(value)
        applied_ref[q] = value.reshape(NEW, SLOTS_DEV, BOX)
    sums = stick_sums(res_ref, applied, halves_ref)
    first = lax.rem(device, 2) == 0
    keep_ref[...] = jnp.where(first, sums[:8], sums[8:])
    give_ref[...] = jnp.where(first, sums[8:], sums[:8])
    inter_ref[...] = in_ref[pl.ds(3, 16, stride=4), :].reshape(2, NEW, RES)


def pair_kernel(keep_ref, came_ref, out_ref):
    out_ref[...] = jnp.broadcast_to((keep_ref[...] + came_ref[...])[None], (DEVICES, 8, 128))


def sum_kernel(in_ref, out_ref):
    for q in range(2):
        total = in_ref[q]
        for i in range(q + 2, DEVICES, 2):
            total = total + in_ref[i]
        out_ref[q] = total


WHOLE = 60000 * 1024
anywhere = pl.BlockSpec(memory_space=pl.ANY)
vmem = pl.BlockSpec(memory_space=pltpu.VMEM)
smem = pl.BlockSpec(memory_space=pltpu.SMEM)


def call(body, out_shape, in_specs, name, scratch=(), limit=24 << 20):
    return pl.pallas_call(
        body,
        out_shape=out_shape,
        in_specs=in_specs,
        out_specs=jax.tree.map(lambda _: vmem, out_shape),
        scratch_shapes=list(scratch),
        name=name,
        compiler_params=pltpu.CompilerParams(vmem_limit_bytes=limit),
        cost_estimate=pl.CostEstimate(flops=0, bytes_accessed=1 << 20, transcendentals=0),
    )


def shaped(shape, dtype=f32):
    return jax.ShapeDtypeStruct(shape, dtype)


def exchange(values, rows):
    values = values.reshape(DEVICES, rows, 128)
    return lax.all_to_all(values, both, split_axis=0, concat_axis=0, tiled=True)


def local(tables, new_bands, resident, potential, stick_pos, stick_count):
    z_table, y_table, to_x, from_x = [jnp.asarray(table) for table in tables]
    resident = jnp.transpose(resident, (0, 2, 3, 1))
    halves_shape = pltpu.VMEM((2, 2, 128, 128), f32)
    sent = call(
        send_kernel, shaped((512, 128)), [smem, vmem, vmem, vmem], "send", scratch=[halves_shape], limit=WHOLE
    )(stick_count, new_bands, resident, z_table)
    came = exchange(sent, 4).reshape(512, 128)
    pick, mask, wide, pot = call(
        place_kernel,
        (
            shaped((2048, 256), bf16),
            shaped((ROWS_X, 2048), bf16),
            shaped((ROWS_X, 2048)),
            shaped((PLANES, BOX, 256)),
        ),
        [vmem, vmem],
        "place",
        limit=WHOLE,
    )(stick_pos.reshape(DEVICES, SLOTS_DEV), potential)
    result = call(
        box_kernel,
        shaped((512, 128)),
        [vmem] + [anywhere] * 7,
        "box",
        scratch=[
            pltpu.VMEM((384, 128), f32),
            pltpu.VMEM((24, 2048), f32),
            pltpu.VMEM((24, 2048), f32),
            pltpu.VMEM((2, 2304, 128), f32),
            pltpu.VMEM((12, 192, 256), bf16),
            pltpu.VMEM((12, 192, 256), bf16),
            pltpu.VMEM((2304, 256), f32),
            pltpu.VMEM((2304, 512), bf16),
            pltpu.VMEM((PLANES, BOX, 256), f32),
            pltpu.VMEM((2048, 256), bf16),
            pltpu.VMEM((ROWS_X, 2048), bf16),
            pltpu.VMEM((ROWS_X, 2048), f32),
            pltpu.VMEM((2, 2, 256, 256), bf16),
            pltpu.VMEM((2, 384, 192), bf16),
            pltpu.VMEM((2, 2, 96, 192), bf16),
            pltpu.SemaphoreType.DMA((7,)),
        ],
        limit=WHOLE,
    )(came, pot, pick, mask, wide, y_table, to_x, from_x)
    returned = exchange(result, 4).reshape(512, 128)
    applied, keep, give, inter = call(
        apply_kernel,
        (
            shaped((2, NEW, SLOTS_DEV, BOX), bf16),
            shaped((8, 128)),
            shaped((8, 128)),
            shaped((2, NEW, RES)),
        ),
        [smem, smem, vmem, vmem, vmem, vmem],
        "apply",
        scratch=[halves_shape],
    )(stick_count, stick_pos, returned, new_bands, resident, z_table)
    other = lax.ppermute(give, "fft", [(i, i ^ 1) for i in range(COLUMNS)])
    partial = call(pair_kernel, shaped((DEVICES, 8, 128)), [vmem, vmem], "pair")(keep, other)
    proj = call(sum_kernel, shaped((2, NEW, RES)), [vmem], "total")(exchange(partial, 8))
    return applied, jnp.transpose(proj, (0, 2, 1)), jnp.transpose(inter, (0, 2, 1))


def solution(mesh):
    return jax.shard_map(
        functools.partial(local, make_tables()),
        mesh=mesh,
        in_specs=(
            P(None, None, both, None),
            P(None, None, both, None),
            P("fft", None, None),
            P(),
            P(both),
        ),
        out_specs=(P(None, None, both, None), P(), P()),
        check_vma=False,
    )
```

```python
import functools

import jax
import jax.numpy as jnp
import ml_dtypes
import numpy as np
from jax import lax
from jax.experimental import pallas as pl
from jax.experimental.pallas import tpu as pltpu
from jax.sharding import PartitionSpec as P

BOX = 192
HALF = 96
SLOTS_DEV = 16
NEW = 8
RES = 128
DEVICES = 128
PLANES = 6
GROUPS = 4
COLUMNS = 32
ROWS_X = 96
f32 = jnp.float32
bf16 = jnp.bfloat16
both = ("band", "fft")
MASK = 2048
TABLES = MASK + 8 * ROWS_X


def halves(table):
    high = table.astype(ml_dtypes.bfloat16)
    low = (table - high.astype(np.float64)).astype(ml_dtypes.bfloat16)
    return high, low


def wave(rows, cols):
    return 2.0 * np.pi / BOX * ((rows[:, None] * cols[None, :]) % BOX)


def rotation(angles):
    return [[np.cos(angles), -np.sin(angles)], [np.sin(angles), np.cos(angles)]]


def make_tables():
    plane = (np.arange(COLUMNS)[None, :] * PLANES + np.arange(PLANES)[:, None]).reshape(-1)
    blocks = rotation(wave(plane, np.arange(BOX)))
    z_table = []
    for q in range(2):
        high, low = halves(np.concatenate([blocks[0][q], blocks[1][q]], axis=0))
        z_table.append(np.concatenate([high, low], axis=0))
    z_table = np.stack(z_table)
    y_table = []
    for odd in range(2):
        blocks = rotation(wave(2 * np.arange(HALF) + odd, np.arange(HALF)))
        full = np.zeros((2, 128, 2, 128))
        for q_in in range(2):
            for q_out in range(2):
                full[q_in, :HALF, q_out, :HALF] = blocks[q_out][q_in]
        y_table.append(np.stack(halves(full.reshape(256, 256))))
    y_table = np.stack(y_table)
    index = np.concatenate([2 * np.arange(48), 2 * np.arange(48) + 1])
    freq = np.where(index < 48, index, index + 96)
    blocks = rotation(wave(np.arange(BOX), freq))
    to_x = np.block(blocks)
    to_x = np.stack(halves(to_x))
    from_x = []
    for odd in range(2):
        angles = -wave(freq[odd * 48 : odd * 48 + 48], np.arange(HALF))
        from_x.append(np.stack(halves(np.block(rotation(angles)))))
    wide = np.concatenate([to_x.reshape(768, BOX), np.stack(from_x).reshape(384, BOX)])
    wide = np.concatenate([wide, np.zeros((1152, 64), wide.dtype)], axis=1)
    return z_table, np.concatenate([y_table.reshape(1024, 256), wide])


def dot(a, b):
    return lax.dot_general(a, b, (((1,), (0,)), ((), ())), preferred_element_type=f32)


def dot_nt(a, b):
    return lax.dot_general(a, b, (((1,), (1,)), ((), ())), preferred_element_type=f32)


def split(values):
    high = values.astype(bf16)
    return high, (values - high.astype(f32)).astype(bf16)


def stick_sums(res_ref, parts, halves_ref):
    for q in range(2):
        halves_ref[q, 0] = parts[q][:, :128].astype(f32)
        halves_ref[q, 1, :, 0:64] = parts[q][:, 128:].astype(f32)
    total = jnp.zeros((16, 128), f32)
    for slot in range(SLOTS_DEV):
        for half, width in ((0, 128), (1, 64)):
            v0 = halves_ref[0, half, pl.ds(slot, 8, stride=16), :][:, :width]
            v1 = halves_ref[1, half, pl.ds(slot, 8, stride=16), :][:, :width]
            rows = slice(half * 128, half * 128 + width)
            total = total + dot(jnp.concatenate([v0, v1], axis=0).astype(bf16), res_ref[0, slot, rows, :])
            total = total + dot(jnp.concatenate([v1, -v0], axis=0).astype(bf16), res_ref[1, slot, rows, :])
    return total


def live_parts(count, nb_ref):
    row = lax.broadcasted_iota(jnp.int32, (NEW * SLOTS_DEV, BOX), 0) & (SLOTS_DEV - 1)
    live = row < count
    return [
        jnp.where(live, nb_ref[q].reshape(NEW * SLOTS_DEV, BOX).astype(f32), 0.0).astype(bf16)
        for q in range(2)
    ]


def send_kernel(count_ref, nb_ref, res_ref, z_ref, out_ref, halves_ref):
    parts = live_parts(count_ref[0], nb_ref)
    acc = dot_nt(z_ref[0], parts[0]) + dot_nt(z_ref[1], parts[1])
    acc = acc[:384] + acc[384:]
    lane = lax.broadcasted_iota(jnp.int32, (COLUMNS, 128), 1) // 32
    for k in range(3):
        for group in range(GROUPS):
            total = jnp.zeros((COLUMNS, 128), f32)
            for c in range(4):
                piece = acc[(k * 4 + c) * 32 : (k * 4 + c + 1) * 32]
                shift = (c - group) * 32 % 128
                if shift:
                    piece = pltpu.roll(piece, shift, 1)
                total = jnp.where(lane == c, piece, total)
            out_ref[pl.ds(group * 128 + k, 32, stride=4), :] = total
    out_ref[pl.ds(3, 16, stride=4), :] = stick_sums(res_ref, parts, halves_ref)
    out_ref[pl.ds(67, 112, stride=4), :] = jnp.zeros((112, 128), f32)


def place_kernel(pos_ref, table_ref, pack_ref):
    pack_ref[MASK + 8 * ROWS_X :, :] = table_ref[...]
    pos = pos_ref[...].astype(f32)
    row = jnp.floor((pos + 0.5) * (1.0 / BOX))
    col = pos - row * BOX
    half = jnp.floor(col * 0.5)
    lane_of = half + (col - 2.0 * half) * 128.0
    row = jnp.where(row < 48.0, row, row - 96.0)
    half = jnp.floor(row * 0.5)
    row = jnp.transpose(half + (row - 2.0 * half) * 48.0)
    lane = lax.broadcasted_iota(jnp.int32, (DEVICES, 256), 1).astype(f32)
    index = lax.broadcasted_iota(jnp.int32, (ROWS_X, 128), 0).astype(f32)
    for slot in range(SLOTS_DEV):
        hit = lane_of[:, slot : slot + 1] == lane
        pack_ref[slot * 128 : (slot + 1) * 128, :] = jnp.where(hit, 1.0, 0.0).astype(bf16)
        hit = jnp.where(jnp.broadcast_to(row[slot : slot + 1, :], (ROWS_X, 128)) == index, 1.0, 0.0)
        start = MASK + slot // 2 * ROWS_X
        pack_ref[start : start + ROWS_X, slot % 2 * 128 : slot % 2 * 128 + 128] = hit.astype(bf16)


CHUNK = 8


def box_kernel(
    in_ref, pot_any, pack_ref, out_ref, flat, high_v, low_v, grid, mid_h, mid_l, back, picked, pot_ref, sem
):
    move = pltpu.make_async_copy(pot_any, pot_ref, sem)
    move.start()

    def y_table(odd, part):
        start = TABLES + (odd * 2 + part) * 256
        return pack_ref[start : start + 256, :]

    def from_x(odd, rows):
        start = TABLES + 1792 + odd * 192
        return pack_ref[start : start + rows, :BOX]

    for k in range(3):
        flat[k * 128 : (k + 1) * 128, :] = jnp.transpose(in_ref[pl.ds(k, 128, stride=4), :])
    for slot in range(SLOTS_DEV):
        lanes = slice(slot * 128, (slot + 1) * 128)
        values = flat[pl.ds(slot, 24, stride=16), :]
        high = values.astype(bf16).astype(f32)
        high_v[:, lanes] = high
        low_v[:, lanes] = values - high

    def scatter(chunk, carry):
        mask = jnp.concatenate(
            [pack_ref[MASK + i * ROWS_X : MASK + (i + 1) * ROWS_X, :] for i in range(8)], axis=1
        )
        start = pl.multiple_of(chunk * (CHUNK * 96), 16)
        for part, source in enumerate((high_v, low_v)):
            blocks = []
            for i in range(CHUNK):
                value = source[pl.ds(chunk * CHUNK + i, 1), :]
                value = jnp.broadcast_to(value, (16, 2048)).astype(bf16)
                blocks.append(mask * jnp.concatenate([value] * 6, axis=0))
            term = dot(jnp.concatenate(blocks, axis=0), pack_ref[0:MASK, :]).astype(bf16)
            for odd in range(2):
                grid[part, odd, pl.ds(start, CHUNK * 96), :] = term[:, odd * 128 : odd * 128 + 128]
        return carry

    lax.fori_loop(0, 24 // CHUNK, scatter, 0)

    for part in range(3):
        outs = []
        for odd in range(2):
            high, low = [
                jnp.concatenate(
                    [grid[i, odd, base + part * 384 : base + part * 384 + 384, :] for base in (0, 1152)], axis=1
                )
                for i in range(2)
            ]
            outs.append(dot(high, y_table(odd, 0)) + dot(low, y_table(odd, 0)) + dot(high, y_table(odd, 1)))
        plus, minus = outs[0] + outs[1], outs[0] - outs[1]
        for q in range(2):
            lanes = slice(q * 128, q * 128 + 128)
            high, low = split(jnp.concatenate([plus[:, lanes], minus[:, lanes]], axis=1))
            for i in range(4):
                for half in range(2):
                    block = (slice(i * 96, i * 96 + 96), slice(half * 128, half * 128 + 128))
                    mid_h[part * 4 + i, half, q * 96 : q * 96 + 96, :] = high[block]
                    mid_l[part * 4 + i, half, q * 96 : q * 96 + 96, :] = low[block]

    move.wait()

    def one_plane(i, weight):
        high = jnp.concatenate([mid_h[i, 0], mid_h[i, 1]], axis=1)
        low = jnp.concatenate([mid_l[i, 0], mid_l[i, 1]], axis=1)
        field = dot(pack_ref[TABLES + 1024 : TABLES + 1792, :BOX], high)
        field = field[:384] + field[384:] + dot(pack_ref[TABLES + 1024 : TABLES + 1408, :BOX], low)
        re, im = field[:192] * weight, field[192:] * weight
        for odd in range(2):
            if odd:
                folded = jnp.concatenate([re[:96] - re[96:], im[:96] - im[96:]], axis=0)
            else:
                folded = jnp.concatenate([re[:96] + re[96:], im[:96] + im[96:]], axis=0)
            high, low = split(folded)
            out = dot(from_x(odd, 192), high)
            out = out[:96] + out[96:] + dot(from_x(odd, 96), low)
            start = pl.multiple_of(i * 96 + odd * 48, 8)
            back[pl.ds(start, 48), :] = out[:48]
            back[pl.ds(start + 1152, 48), :] = out[48:]

    def plane(p, carry):
        value = pot_ref[p]
        gap = jnp.zeros((BOX, 32), f32)
        weight = jnp.concatenate([value[:, :HALF], gap, value[:, HALF:], gap], axis=1)
        for i in range(2):
            one_plane(2 * p + i, weight)
        return carry

    lax.fori_loop(0, PLANES, plane, 0, unroll=2)

    for part in range(4):
        re = back[part * 288 : part * 288 + 288, :]
        im = back[1152 + part * 288 : 1152 + part * 288 + 288, :]
        outs = []
        for odd in range(2):
            if odd:
                pair = [re[:, :128] - re[:, 128:], im[:, :128] - im[:, 128:]]
            else:
                pair = [re[:, :128] + re[:, 128:], im[:, :128] + im[:, 128:]]
            high, low = split(jnp.concatenate(pair, axis=1))
            outs.append(
                dot_nt(high, y_table(odd, 0)) + dot_nt(low, y_table(odd, 0)) + dot_nt(high, y_table(odd, 1))
            )
        for q in range(2):
            lanes = slice(q * 128, q * 128 + 128)
            start = q * 1152 + part * 288
            for odd in range(2):
                high, low = split(outs[odd][:, lanes])
                picked[odd, start : start + 288, :] = high
                picked[2 + odd, start : start + 288, :] = low

    def pick(tile, carry):
        start = pl.multiple_of(tile * 256, 256)
        sel = pack_ref[pl.ds(start, 256), :]
        mask = pack_ref[pl.ds(pl.multiple_of(MASK + tile * ROWS_X, 32), ROWS_X), :].astype(f32)
        size = 2304 // 2
        totals = []
        for i in range(2):
            rows = slice(i * size, i * size + size)
            out = dot_nt(jnp.concatenate([picked[0, rows], picked[1, rows]], axis=1), sel)
            out = out + dot_nt(jnp.concatenate([picked[2, rows], picked[3, rows]], axis=1), sel)
            totals.append(jnp.sum(out.reshape(size // ROWS_X, ROWS_X, 256) * mask[None], axis=1))
        total = jnp.concatenate(totals, axis=0)
        flat[pl.ds(2 * tile, 24, stride=16), :] = total[:, :128]
        flat[pl.ds(2 * tile + 1, 24, stride=16), :] = total[:, 128:]
        return carry

    lax.fori_loop(0, 8, pick, 0, unroll=4)

    for k in range(3):
        out_ref[pl.ds(k, 128, stride=4), :] = jnp.transpose(flat[k * 128 : (k + 1) * 128, :])
    total = jnp.sum(in_ref[pl.ds(3, 128, stride=4), :], axis=0, keepdims=True)
    out_ref[pl.ds(3, 128, stride=4), :] = jnp.broadcast_to(total, (DEVICES, 128))


def apply_kernel(
    count_ref, pos_ref, in_ref, nb_ref, res_ref, z_ref, applied_ref, keep_ref, give_ref, inter_ref,
    halves_ref,
):
    device = lax.axis_index("band") * COLUMNS + lax.axis_index("fft")
    lane = lax.broadcasted_iota(jnp.int32, (COLUMNS, 128), 1) // 32
    pieces = []
    for k in range(3):
        for c in range(4):
            total = jnp.zeros((COLUMNS, 128), f32)
            for group in range(GROUPS):
                piece = in_ref[pl.ds(group * 128 + k, 32, stride=4), :]
                shift = (group - c) * 32 % 128
                if shift:
                    piece = pltpu.roll(piece, shift, 1)
                total = jnp.where(lane == group, piece, total)
            pieces.append(total)
    field = jnp.transpose(jnp.concatenate(pieces, axis=0))
    high, low = split(field)
    parts = live_parts(count_ref[0], nb_ref)
    row = lax.broadcasted_iota(jnp.int32, (NEW * SLOTS_DEV, BOX), 0) & (SLOTS_DEV - 1)
    squares = jnp.zeros((NEW * SLOTS_DEV, BOX), f32)
    for slot in range(SLOTS_DEV):
        pos = pos_ref[device * SLOTS_DEV + slot]
        kx = lax.div(pos, jnp.int32(BOX))
        ky = pos - kx * BOX
        kx = jnp.where(kx < HALF, kx, kx - BOX)
        ky = jnp.where(ky < HALF, ky, ky - BOX)
        squares = jnp.where(row == slot, (kx * kx + ky * ky).astype(f32), squares)
    kz = lax.broadcasted_iota(jnp.int32, (NEW * SLOTS_DEV, BOX), 1)
    kz = jnp.where(kz < HALF, kz, kz - BOX).astype(f32)
    kinetic = 2.0 * (squares + kz * kz) / float(BOX * BOX)
    live = row < count_ref[0]
    applied = []
    for q in range(2):
        table = z_ref[q]
        spectrum = dot(high, table[:384]) + dot(low, table[:384]) + dot(high, table[384:])
        spectrum = spectrum * (1.0 / BOX**3)
        value = jnp.where(live, kinetic * parts[q].astype(f32) + spectrum, 0.0).astype(bf16)
        applied.append(value)
        applied_ref[q] = value.reshape(NEW, SLOTS_DEV, BOX)
    sums = stick_sums(res_ref, applied, halves_ref)
    first = lax.rem(device, 2) == 0
    keep_ref[...] = jnp.where(first, sums[:8], sums[8:])
    give_ref[...] = jnp.where(first, sums[8:], sums[:8])
    inter_ref[...] = in_ref[pl.ds(3, 16, stride=4), :].reshape(2, NEW, RES)


def pair_kernel(keep_ref, came_ref, out_ref):
    total = keep_ref[...] + came_ref[...]
    out_ref[...] = jnp.broadcast_to(total[None], (DEVICES // 2, 8, 128)).reshape(512, 128)


def sum_kernel(in_ref, out_ref):
    total = in_ref[0:8, :]
    for i in range(8, 512, 8):
        total = total + in_ref[i : i + 8, :]
    out_ref[...] = total


def join_kernel(mine_ref, other_ref, out_ref):
    first = lax.rem(lax.axis_index("fft"), 2) == 0
    mine, other = mine_ref[...], other_ref[...]
    low = jnp.where(first, mine, other)
    high = jnp.where(first, other, mine)
    for q in range(2):
        rows = slice(q * 4, q * 4 + 4)
        out_ref[q] = jnp.concatenate([low[rows], high[rows]], axis=0)


WHOLE = 60000 * 1024
vmem = pl.BlockSpec(memory_space=pltpu.VMEM)
smem = pl.BlockSpec(memory_space=pltpu.SMEM)


def call(body, out_shape, in_specs, name, scratch=(), limit=24 << 20):
    return pl.pallas_call(
        body,
        out_shape=out_shape,
        in_specs=in_specs,
        out_specs=jax.tree.map(lambda _: vmem, out_shape),
        scratch_shapes=list(scratch),
        name=name,
        compiler_params=pltpu.CompilerParams(vmem_limit_bytes=limit),
        cost_estimate=pl.CostEstimate(flops=0, bytes_accessed=1 << 20, transcendentals=0),
    )


def shaped(shape, dtype=f32):
    return jax.ShapeDtypeStruct(shape, dtype)


def exchange(values, rows):
    values = values.reshape(DEVICES, rows, 128)
    return lax.all_to_all(values, both, split_axis=0, concat_axis=0, tiled=True)


def local(tables, new_bands, resident, potential, stick_pos, stick_count):
    z_table, box_tables = [jnp.asarray(table) for table in tables]
    resident = jnp.transpose(resident, (0, 2, 3, 1))
    halves_shape = pltpu.VMEM((2, 2, 128, 128), f32)
    sent = call(
        send_kernel, shaped((512, 128)), [smem, vmem, vmem, vmem], "send", scratch=[halves_shape], limit=WHOLE
    )(stick_count, new_bands, resident, z_table)
    came = exchange(sent, 4).reshape(512, 128)
    pack = call(
        place_kernel,
        shaped((TABLES + 2176, 256), bf16),
        [vmem] * 2,
        "place",
        limit=16 << 20,
    )(stick_pos.reshape(DEVICES, SLOTS_DEV), box_tables)
    result = call(
        box_kernel,
        shaped((512, 128)),
        [vmem, pl.BlockSpec(memory_space=pltpu.HBM), vmem],
        "box",
        scratch=[
            pltpu.VMEM((384, 128), f32),
            pltpu.VMEM((24, 2048), f32),
            pltpu.VMEM((24, 2048), f32),
            pltpu.VMEM((2, 2, 2304, 128), bf16),
            pltpu.VMEM((12, 2, 192, 128), bf16),
            pltpu.VMEM((12, 2, 192, 128), bf16),
            pltpu.VMEM((2304, 256), f32),
            pltpu.VMEM((4, 2304, 128), bf16),
            pltpu.VMEM((PLANES, BOX, BOX), f32),
            pltpu.SemaphoreType.DMA,
        ],
        limit=40 << 20,
    )(came, pltpu.with_memory_space_constraint(potential, pltpu.HBM), pack)
    returned = exchange(result, 4).reshape(512, 128)
    applied, keep, give, inter = call(
        apply_kernel,
        (
            shaped((2, NEW, SLOTS_DEV, BOX), bf16),
            shaped((8, 128)),
            shaped((8, 128)),
            shaped((2, NEW, RES)),
        ),
        [smem, smem, vmem, vmem, vmem, vmem],
        "apply",
        scratch=[halves_shape],
    )(stick_count, stick_pos, returned, new_bands, resident, z_table)
    pairs = [(i, i ^ 1) for i in range(COLUMNS)]
    other = lax.ppermute(give, "fft", pairs)
    partial = call(pair_kernel, shaped((512, 128)), [vmem, vmem], "pair")(keep, other)
    mine = call(sum_kernel, shaped((8, 128)), [vmem], "total")(exchange(partial, 4).reshape(512, 128))
    other = lax.ppermute(mine, "fft", pairs)
    proj = call(join_kernel, shaped((2, NEW, RES)), [vmem, vmem], "join")(mine, other)
    return applied, jnp.transpose(proj, (0, 2, 1)), jnp.transpose(inter, (0, 2, 1))


def solution(mesh):
    return jax.shard_map(
        functools.partial(local, make_tables()),
        mesh=mesh,
        in_specs=(
            P(None, None, both, None),
            P(None, None, both, None),
            P("fft", None, None),
            P(),
            P(both),
        ),
        out_specs=(P(None, None, both, None), P(), P()),
        check_vma=False,
    )
```

```python
import functools

import jax
import jax.numpy as jnp
import ml_dtypes
import numpy as np
from jax import lax
from jax.experimental import pallas as pl
from jax.experimental.pallas import tpu as pltpu
from jax.sharding import PartitionSpec as P

BOX = 192
HALF = 96
SLOTS_DEV = 16
NEW = 8
RES = 128
DEVICES = 128
PLANES = 6
GROUPS = 4
COLUMNS = 32
ROWS = 72
f32 = jnp.float32
bf16 = jnp.bfloat16
both = ("band", "fft")
MASK = 2048
TABLES = MASK + 8 * 2 * ROWS


def halves(table):
    high = table.astype(ml_dtypes.bfloat16)
    low = (table - high.astype(np.float64)).astype(ml_dtypes.bfloat16)
    return high, low


def wave(rows, cols):
    return 2.0 * np.pi / BOX * ((rows[:, None] * cols[None, :]) % BOX)


def rotation(angles):
    return [[np.cos(angles), -np.sin(angles)], [np.sin(angles), np.cos(angles)]]


def make_tables():
    plane = (np.arange(COLUMNS)[None, :] * PLANES + np.arange(PLANES)[:, None]).reshape(-1)
    blocks = rotation(wave(plane, np.arange(BOX)))
    z_table = []
    for q in range(2):
        high, low = halves(np.concatenate([blocks[0][q], blocks[1][q]], axis=0))
        z_table.append(np.concatenate([high, low], axis=0))
    z_table = np.stack(z_table)
    y_table = []
    for odd in range(2):
        blocks = rotation(wave(2 * np.arange(HALF) + odd, np.arange(HALF)))
        full = np.zeros((2, 128, 2, 128))
        for q_in in range(2):
            for q_out in range(2):
                full[q_in, :HALF, q_out, :HALF] = blocks[q_out][q_in]
        y_table.append(np.stack(halves(full.reshape(256, 256))))
    y_table = np.stack(y_table)
    index = np.concatenate([2 * np.arange(48), 2 * np.arange(48) + 1])
    freq = np.where(index < 48, index, index + 96)
    blocks = rotation(wave(np.arange(BOX), freq))
    to_x = np.block(blocks)
    to_x = np.stack(halves(to_x))
    from_x = []
    for odd in range(2):
        angles = -wave(freq[odd * 48 : odd * 48 + 48], np.arange(HALF))
        from_x.append(np.stack(halves(np.block(rotation(angles)))))
    wide = np.concatenate([to_x.reshape(768, BOX), np.stack(from_x).reshape(384, BOX)])
    wide = np.concatenate([wide, np.zeros((1152, 64), wide.dtype)], axis=1)
    return z_table, np.concatenate([y_table.reshape(1024, 256), wide])


def dot(a, b):
    return lax.dot_general(a, b, (((1,), (0,)), ((), ())), preferred_element_type=f32)


def dot_nt(a, b):
    return lax.dot_general(a, b, (((1,), (1,)), ((), ())), preferred_element_type=f32)


def split(values):
    high = values.astype(bf16)
    return high, (values - high.astype(f32)).astype(bf16)


def stick_sums(res_ref, parts, halves_ref):
    for q in range(2):
        halves_ref[q, 0] = parts[q][:, :128].astype(f32)
        halves_ref[q, 1, :, 0:64] = parts[q][:, 128:].astype(f32)
    total = jnp.zeros((16, 128), f32)
    for slot in range(SLOTS_DEV):
        for half, width in ((0, 128), (1, 64)):
            v0 = halves_ref[0, half, pl.ds(slot, 8, stride=16), :][:, :width]
            v1 = halves_ref[1, half, pl.ds(slot, 8, stride=16), :][:, :width]
            rows = slice(half * 128, half * 128 + width)
            total = total + dot(jnp.concatenate([v0, v1], axis=0).astype(bf16), res_ref[0, slot, rows, :])
            total = total + dot(jnp.concatenate([v1, -v0], axis=0).astype(bf16), res_ref[1, slot, rows, :])
    return total


def live_parts(count, nb_ref):
    row = lax.broadcasted_iota(jnp.int32, (NEW * SLOTS_DEV, BOX), 0) & (SLOTS_DEV - 1)
    live = row < count
    return [
        jnp.where(live, nb_ref[q].reshape(NEW * SLOTS_DEV, BOX).astype(f32), 0.0).astype(bf16)
        for q in range(2)
    ]


def send_kernel(count_ref, nb_ref, res_ref, z_ref, out_ref, halves_ref):
    parts = live_parts(count_ref[0], nb_ref)
    acc = dot_nt(z_ref[0], parts[0]) + dot_nt(z_ref[1], parts[1])
    acc = acc[:384] + acc[384:]
    lane = lax.broadcasted_iota(jnp.int32, (COLUMNS, 128), 1) // 32
    for k in range(3):
        for group in range(GROUPS):
            total = jnp.zeros((COLUMNS, 128), f32)
            for c in range(4):
                piece = acc[(k * 4 + c) * 32 : (k * 4 + c + 1) * 32]
                shift = (c - group) * 32 % 128
                if shift:
                    piece = pltpu.roll(piece, shift, 1)
                total = jnp.where(lane == c, piece, total)
            out_ref[pl.ds(group * 128 + k, 32, stride=4), :] = total
    out_ref[pl.ds(3, 16, stride=4), :] = stick_sums(res_ref, parts, halves_ref)
    out_ref[pl.ds(67, 112, stride=4), :] = jnp.zeros((112, 128), f32)


def place_kernel(pos_ref, table_ref, pack_ref):
    pack_ref[TABLES:, :] = table_ref[...]
    pos = pos_ref[...].astype(f32)
    row = jnp.floor((pos + 0.5) * (1.0 / BOX))
    col = pos - row * BOX
    cell = jnp.floor(col * 0.5)
    side = (col - 2.0 * cell) * 128.0
    row = jnp.where(row < 48.0, row, row - 96.0)
    half = jnp.floor(row * 0.5)
    row = half + (row - 2.0 * half) * 48.0
    third = jnp.floor((cell + 0.5) * (1.0 / 32.0))
    lane_of = side + jnp.where(row < 72.0, cell, 96.0 + cell - 32.0 * third)
    row = jnp.transpose(jnp.where(row < 72.0, row, row - 72.0 + 24.0 * third))
    lane = lax.broadcasted_iota(jnp.int32, (DEVICES, 256), 1).astype(f32)
    index = lax.broadcasted_iota(jnp.int32, (2 * ROWS, 128), 0)
    index = jnp.where(index < ROWS, index, index - ROWS).astype(f32)
    for slot in range(SLOTS_DEV):
        hit = lane_of[:, slot : slot + 1] == lane
        pack_ref[slot * 128 : (slot + 1) * 128, :] = jnp.where(hit, 1.0, 0.0).astype(bf16)
        hit = jnp.broadcast_to(row[slot : slot + 1, :], (2 * ROWS, 128)) == index
        start = MASK + slot // 2 * 2 * ROWS
        lanes = slice(slot % 2 * 128, slot % 2 * 128 + 128)
        pack_ref[start : start + 2 * ROWS, lanes] = jnp.where(hit, 1.0, 0.0).astype(bf16)


def unfold(block):
    lane = lax.broadcasted_iota(jnp.int32, (24, 128), 1)
    last = pltpu.roll(block[48:72], 96, 1)
    last = jnp.where(lane < 64, pltpu.roll(block[24:48], 64, 1), last)
    last = jnp.where(lane < 32, pltpu.roll(block[:24], 32, 1), last)
    return jnp.concatenate([block, last], axis=0)


def fold(block):
    lane = lax.broadcasted_iota(jnp.int32, (24, 128), 1)
    thirds = [
        jnp.where(lane < 96, block[i * 24 : i * 24 + 24], pltpu.roll(block[72:96], 96 - 32 * i, 1))
        for i in range(3)
    ]
    return jnp.concatenate(thirds, axis=0)


CHUNK = 8


def box_kernel(
    in_ref, pot_any, pack_ref, out_ref, flat, high_v, low_v, grid, mid_h, mid_l, back, picked, pot_ref, sem
):
    move = pltpu.make_async_copy(pot_any, pot_ref, sem)
    move.start()

    def y_table(odd, part):
        start = TABLES + (odd * 2 + part) * 256
        return pack_ref[start : start + 256, :]

    def from_x(odd, rows):
        start = TABLES + 1792 + odd * 192
        return pack_ref[start : start + rows, :BOX]

    for k in range(3):
        flat[k * 128 : (k + 1) * 128, :] = jnp.transpose(in_ref[pl.ds(k, 128, stride=4), :])
    for slot in range(SLOTS_DEV):
        lanes = slice(slot * 128, (slot + 1) * 128)
        values = flat[pl.ds(slot, 24, stride=16), :]
        high = values.astype(bf16).astype(f32)
        high_v[:, lanes] = high
        low_v[:, lanes] = values - high

    def scatter(chunk, carry):
        mask = jnp.concatenate(
            [pack_ref[MASK + i * 2 * ROWS : MASK + (i + 1) * 2 * ROWS, :] for i in range(8)], axis=1
        )
        start = pl.multiple_of(chunk * (CHUNK * 96), 16)
        for part, source in enumerate((high_v, low_v)):
            blocks = []
            for i in range(0, CHUNK, 2):
                first = jnp.broadcast_to(source[pl.ds(chunk * CHUNK + i, 1), :], (8, 2048))
                second = jnp.broadcast_to(source[pl.ds(chunk * CHUNK + i + 1, 1), :], (8, 2048))
                upper = jnp.concatenate([first, first], axis=0).astype(bf16)
                middle = jnp.concatenate([first, second], axis=0).astype(bf16)
                lower = jnp.concatenate([second, second], axis=0).astype(bf16)
                blocks.append(mask * jnp.concatenate([upper] * 4 + [middle] + [lower] * 4, axis=0))
            term = dot(jnp.concatenate(blocks, axis=0), pack_ref[0:MASK, :])
            for odd in range(2):
                for i in range(CHUNK):
                    block = unfold(term[i * ROWS : (i + 1) * ROWS, odd * 128 : odd * 128 + 128])
                    grid[part, odd, pl.ds(start + i * 96, 96), :] = block.astype(bf16)
        return carry

    lax.fori_loop(0, 24 // CHUNK, scatter, 0)

    for part in range(3):
        outs = []
        for odd in range(2):
            high, low = [
                jnp.concatenate(
                    [grid[i, odd, base + part * 384 : base + part * 384 + 384, :] for base in (0, 1152)], axis=1
                )
                for i in range(2)
            ]
            outs.append(dot(high, y_table(odd, 0)) + dot(low, y_table(odd, 0)) + dot(high, y_table(odd, 1)))
        plus, minus = outs[0] + outs[1], outs[0] - outs[1]
        for q in range(2):
            lanes = slice(q * 128, q * 128 + 128)
            high, low = split(jnp.concatenate([plus[:, lanes], minus[:, lanes]], axis=1))
            for i in range(4):
                for half in range(2):
                    block = (slice(i * 96, i * 96 + 96), slice(half * 128, half * 128 + 128))
                    mid_h[part * 4 + i, half, q * 96 : q * 96 + 96, :] = high[block]
                    mid_l[part * 4 + i, half, q * 96 : q * 96 + 96, :] = low[block]

    move.wait()

    def one_plane(i, weight):
        high = jnp.concatenate([mid_h[i, 0], mid_h[i, 1]], axis=1)
        low = jnp.concatenate([mid_l[i, 0], mid_l[i, 1]], axis=1)
        field = dot(pack_ref[TABLES + 1024 : TABLES + 1792, :BOX], high)
        field = field[:384] + field[384:] + dot(pack_ref[TABLES + 1024 : TABLES + 1408, :BOX], low)
        re, im = field[:192] * weight, field[192:] * weight
        for odd in range(2):
            if odd:
                folded = jnp.concatenate([re[:96] - re[96:], im[:96] - im[96:]], axis=0)
            else:
                folded = jnp.concatenate([re[:96] + re[96:], im[:96] + im[96:]], axis=0)
            high, low = split(folded)
            out = dot(from_x(odd, 192), high)
            out = out[:96] + out[96:] + dot(from_x(odd, 96), low)
            start = pl.multiple_of(i * 96 + odd * 48, 8)
            back[pl.ds(start, 48), :] = out[:48]
            back[pl.ds(start + 1152, 48), :] = out[48:]

    def plane(p, carry):
        value = pot_ref[p]
        gap = jnp.zeros((BOX, 32), f32)
        weight = jnp.concatenate([value[:, :HALF], gap, value[:, HALF:], gap], axis=1)
        for i in range(2):
            one_plane(2 * p + i, weight)
        return carry

    lax.fori_loop(0, PLANES, plane, 0, unroll=2)

    for part in range(4):
        re = back[part * 288 : part * 288 + 288, :]
        im = back[1152 + part * 288 : 1152 + part * 288 + 288, :]
        outs = []
        for odd in range(2):
            if odd:
                pair = [re[:, :128] - re[:, 128:], im[:, :128] - im[:, 128:]]
            else:
                pair = [re[:, :128] + re[:, 128:], im[:, :128] + im[:, 128:]]
            high, low = split(jnp.concatenate(pair, axis=1))
            outs.append(
                dot_nt(high, y_table(odd, 0)) + dot_nt(low, y_table(odd, 0)) + dot_nt(high, y_table(odd, 1))
            )
        for q in range(2):
            lanes = slice(q * 128, q * 128 + 128)
            start = q * 12 * ROWS + part * 3 * ROWS
            for odd in range(2):
                rows = [fold(outs[odd][i * 96 : i * 96 + 96, lanes]) for i in range(3)]
                high, low = split(jnp.concatenate(rows, axis=0))
                picked[odd, start : start + 3 * ROWS, :] = high
                picked[2 + odd, start : start + 3 * ROWS, :] = low

    def pick(tile, carry):
        start = pl.multiple_of(tile * 256, 256)
        sel = pack_ref[pl.ds(start, 256), :]
        mask = pack_ref[pl.ds(pl.multiple_of(MASK + tile * 2 * ROWS, 16), 2 * ROWS), :].astype(f32)[:ROWS]
        size = 12 * ROWS
        totals = []
        for i in range(2):
            rows = slice(i * size, i * size + size)
            out = dot_nt(jnp.concatenate([picked[0, rows], picked[1, rows]], axis=1), sel)
            out = out + dot_nt(jnp.concatenate([picked[2, rows], picked[3, rows]], axis=1), sel)
            totals.append(jnp.sum(out.reshape(12, ROWS, 256) * mask[None], axis=1))
        total = jnp.concatenate(totals, axis=0)
        flat[pl.ds(2 * tile, 24, stride=16), :] = total[:, :128]
        flat[pl.ds(2 * tile + 1, 24, stride=16), :] = total[:, 128:]
        return carry

    lax.fori_loop(0, 8, pick, 0, unroll=4)

    for k in range(3):
        out_ref[pl.ds(k, 128, stride=4), :] = jnp.transpose(flat[k * 128 : (k + 1) * 128, :])
    total = jnp.sum(in_ref[pl.ds(3, 128, stride=4), :], axis=0, keepdims=True)
    out_ref[pl.ds(3, 128, stride=4), :] = jnp.broadcast_to(total, (DEVICES, 128))


def apply_kernel(
    count_ref, pos_ref, in_ref, nb_ref, res_ref, z_ref, applied_ref, keep_ref, give_ref, inter_ref,
    halves_ref,
):
    device = lax.axis_index("band") * COLUMNS + lax.axis_index("fft")
    lane = lax.broadcasted_iota(jnp.int32, (COLUMNS, 128), 1) // 32
    pieces = []
    for k in range(3):
        for c in range(4):
            total = jnp.zeros((COLUMNS, 128), f32)
            for group in range(GROUPS):
                piece = in_ref[pl.ds(group * 128 + k, 32, stride=4), :]
                shift = (group - c) * 32 % 128
                if shift:
                    piece = pltpu.roll(piece, shift, 1)
                total = jnp.where(lane == group, piece, total)
            pieces.append(total)
    field = jnp.transpose(jnp.concatenate(pieces, axis=0))
    high, low = split(field)
    parts = live_parts(count_ref[0], nb_ref)
    row = lax.broadcasted_iota(jnp.int32, (NEW * SLOTS_DEV, BOX), 0) & (SLOTS_DEV - 1)
    squares = jnp.zeros((NEW * SLOTS_DEV, BOX), f32)
    for slot in range(SLOTS_DEV):
        pos = pos_ref[device * SLOTS_DEV + slot]
        kx = lax.div(pos, jnp.int32(BOX))
        ky = pos - kx * BOX
        kx = jnp.where(kx < HALF, kx, kx - BOX)
        ky = jnp.where(ky < HALF, ky, ky - BOX)
        squares = jnp.where(row == slot, (kx * kx + ky * ky).astype(f32), squares)
    kz = lax.broadcasted_iota(jnp.int32, (NEW * SLOTS_DEV, BOX), 1)
    kz = jnp.where(kz < HALF, kz, kz - BOX).astype(f32)
    kinetic = 2.0 * (squares + kz * kz) / float(BOX * BOX)
    live = row < count_ref[0]
    applied = []
    for q in range(2):
        table = z_ref[q]
        spectrum = dot(high, table[:384]) + dot(low, table[:384]) + dot(high, table[384:])
        spectrum = spectrum * (1.0 / BOX**3)
        value = jnp.where(live, kinetic * parts[q].astype(f32) + spectrum, 0.0).astype(bf16)
        applied.append(value)
        applied_ref[q] = value.reshape(NEW, SLOTS_DEV, BOX)
    sums = stick_sums(res_ref, applied, halves_ref)
    first = lax.rem(device, 2) == 0
    keep_ref[...] = jnp.where(first, sums[:8], sums[8:])
    give_ref[...] = jnp.where(first, sums[8:], sums[:8])
    inter_ref[...] = in_ref[pl.ds(3, 16, stride=4), :].reshape(2, NEW, RES)


def pair_kernel(keep_ref, came_ref, out_ref):
    total = keep_ref[...] + came_ref[...]
    out_ref[...] = jnp.broadcast_to(total[None], (DEVICES // 2, 8, 128)).reshape(512, 128)


def sum_kernel(in_ref, out_ref):
    total = in_ref[0:8, :]
    for i in range(8, 512, 8):
        total = total + in_ref[i : i + 8, :]
    out_ref[...] = total


def join_kernel(mine_ref, other_ref, out_ref):
    first = lax.rem(lax.axis_index("fft"), 2) == 0
    mine, other = mine_ref[...], other_ref[...]
    low = jnp.where(first, mine, other)
    high = jnp.where(first, other, mine)
    for q in range(2):
        rows = slice(q * 4, q * 4 + 4)
        out_ref[q] = jnp.concatenate([low[rows], high[rows]], axis=0)


WHOLE = 60000 * 1024
vmem = pl.BlockSpec(memory_space=pltpu.VMEM)
smem = pl.BlockSpec(memory_space=pltpu.SMEM)


def call(body, out_shape, in_specs, name, scratch=(), limit=24 << 20):
    return pl.pallas_call(
        body,
        out_shape=out_shape,
        in_specs=in_specs,
        out_specs=jax.tree.map(lambda _: vmem, out_shape),
        scratch_shapes=list(scratch),
        name=name,
        compiler_params=pltpu.CompilerParams(vmem_limit_bytes=limit),
        cost_estimate=pl.CostEstimate(flops=0, bytes_accessed=1 << 20, transcendentals=0),
    )


def shaped(shape, dtype=f32):
    return jax.ShapeDtypeStruct(shape, dtype)


def exchange(values, rows):
    values = values.reshape(DEVICES, rows, 128)
    return lax.all_to_all(values, both, split_axis=0, concat_axis=0, tiled=True)


def local(tables, new_bands, resident, potential, stick_pos, stick_count):
    z_table, box_tables = [jnp.asarray(table) for table in tables]
    resident = jnp.transpose(resident, (0, 2, 3, 1))
    halves_shape = pltpu.VMEM((2, 2, 128, 128), f32)
    sent = call(
        send_kernel, shaped((512, 128)), [smem, vmem, vmem, vmem], "send", scratch=[halves_shape], limit=WHOLE
    )(stick_count, new_bands, resident, z_table)
    came = exchange(sent, 4).reshape(512, 128)
    pack = call(
        place_kernel,
        shaped((TABLES + 2176, 256), bf16),
        [vmem] * 2,
        "place",
        limit=16 << 20,
    )(stick_pos.reshape(DEVICES, SLOTS_DEV), box_tables)
    result = call(
        box_kernel,
        shaped((512, 128)),
        [vmem, pl.BlockSpec(memory_space=pltpu.HBM), vmem],
        "box",
        scratch=[
            pltpu.VMEM((384, 128), f32),
            pltpu.VMEM((24, 2048), f32),
            pltpu.VMEM((24, 2048), f32),
            pltpu.VMEM((2, 2, 2304, 128), bf16),
            pltpu.VMEM((12, 2, 192, 128), bf16),
            pltpu.VMEM((12, 2, 192, 128), bf16),
            pltpu.VMEM((2304, 256), f32),
            pltpu.VMEM((4, 24 * ROWS, 128), bf16),
            pltpu.VMEM((PLANES, BOX, BOX), f32),
            pltpu.SemaphoreType.DMA,
        ],
        limit=40 << 20,
    )(came, pltpu.with_memory_space_constraint(potential, pltpu.HBM), pack)
    returned = exchange(result, 4).reshape(512, 128)
    applied, keep, give, inter = call(
        apply_kernel,
        (
            shaped((2, NEW, SLOTS_DEV, BOX), bf16),
            shaped((8, 128)),
            shaped((8, 128)),
            shaped((2, NEW, RES)),
        ),
        [smem, smem, vmem, vmem, vmem, vmem],
        "apply",
        scratch=[halves_shape],
    )(stick_count, stick_pos, returned, new_bands, resident, z_table)
    pairs = [(i, i ^ 1) for i in range(COLUMNS)]
    other = lax.ppermute(give, "fft", pairs)
    partial = call(pair_kernel, shaped((512, 128)), [vmem, vmem], "pair")(keep, other)
    mine = call(sum_kernel, shaped((8, 128)), [vmem], "total")(exchange(partial, 4).reshape(512, 128))
    other = lax.ppermute(mine, "fft", pairs)
    proj = call(join_kernel, shaped((2, NEW, RES)), [vmem, vmem], "join")(mine, other)
    return applied, jnp.transpose(proj, (0, 2, 1)), jnp.transpose(inter, (0, 2, 1))


def solution(mesh):
    return jax.shard_map(
        functools.partial(local, make_tables()),
        mesh=mesh,
        in_specs=(
            P(None, None, both, None),
            P(None, None, both, None),
            P("fft", None, None),
            P(),
            P(both),
        ),
        out_specs=(P(None, None, both, None), P(), P()),
        check_vma=False,
    )
```

```python
import functools

import jax
import jax.numpy as jnp
import ml_dtypes
import numpy as np
from jax import lax
from jax.experimental import pallas as pl
from jax.experimental.pallas import tpu as pltpu
from jax.sharding import PartitionSpec as P

BOX = 192
HALF = 96
SLOTS_DEV = 16
NEW = 8
RES = 128
DEVICES = 128
PLANES = 6
GROUPS = 4
COLUMNS = 32
ROWS = 72
f32 = jnp.float32
bf16 = jnp.bfloat16
both = ("band", "fft")
MASK = 2048
TABLES = MASK + 8 * 2 * ROWS


def halves(table):
    high = table.astype(ml_dtypes.bfloat16)
    low = (table - high.astype(np.float64)).astype(ml_dtypes.bfloat16)
    return high, low


def wave(rows, cols):
    return 2.0 * np.pi / BOX * ((rows[:, None] * cols[None, :]) % BOX)


def rotation(angles):
    return [[np.cos(angles), -np.sin(angles)], [np.sin(angles), np.cos(angles)]]


def make_tables():
    plane = (np.arange(COLUMNS)[None, :] * PLANES + np.arange(PLANES)[:, None]).reshape(-1)
    blocks = rotation(wave(plane, np.arange(BOX)))
    z_table = []
    for q in range(2):
        high, low = halves(np.concatenate([blocks[0][q], blocks[1][q]], axis=0))
        z_table.append(np.concatenate([high, low], axis=0))
    z_table = np.stack(z_table)
    y_table = []
    for odd in range(2):
        blocks = rotation(wave(2 * np.arange(HALF) + odd, np.arange(HALF)))
        full = np.zeros((2, 128, 2, 128))
        for q_in in range(2):
            for q_out in range(2):
                full[q_in, :HALF, q_out, :HALF] = blocks[q_out][q_in]
        y_table.append(np.stack(halves(full.reshape(256, 256))))
    y_table = np.stack(y_table)
    index = np.concatenate([2 * np.arange(48), 2 * np.arange(48) + 1])
    freq = np.where(index < 48, index, index + 96)
    blocks = rotation(wave(np.arange(BOX), freq))
    to_x = np.block(blocks)
    to_x = np.stack(halves(to_x))
    from_x = []
    for odd in range(2):
        angles = -wave(freq[odd * 48 : odd * 48 + 48], np.arange(HALF))
        from_x.append(np.stack(halves(np.block(rotation(angles)))))
    wide = np.concatenate([to_x.reshape(768, BOX), np.stack(from_x).reshape(384, BOX)])
    wide = np.concatenate([wide, np.zeros((1152, 64), wide.dtype)], axis=1)
    return z_table, np.concatenate([y_table.reshape(1024, 256), wide])


def dot(a, b):
    return lax.dot_general(a, b, (((1,), (0,)), ((), ())), preferred_element_type=f32)


def dot_nt(a, b):
    return lax.dot_general(a, b, (((1,), (1,)), ((), ())), preferred_element_type=f32)


def split(values):
    high = values.astype(bf16)
    return high, (values - high.astype(f32)).astype(bf16)


def stick_sums(res_ref, parts, halves_ref):
    for q in range(2):
        halves_ref[q, 0] = parts[q][:, :128].astype(f32)
        halves_ref[q, 1, :, 0:64] = parts[q][:, 128:].astype(f32)
    totals = [jnp.zeros((32, 256), f32)] * 2
    for slot in range(SLOTS_DEV):
        v0, v1 = [
            jnp.concatenate(
                [halves_ref[q, half, pl.ds(slot, 8, stride=16), :][:, :width] for half, width in ((0, 128), (1, 64))],
                axis=1,
            )
            for q in range(2)
        ]
        left = jnp.concatenate([v0, v1, v1, -v0], axis=0).astype(bf16)
        right = jnp.concatenate([res_ref[0, slot], res_ref[1, slot]], axis=1)
        totals[slot % 2] = totals[slot % 2] + dot(left, right)
    total = sum(totals[1:], totals[0])
    return total[:16, :128] + total[16:, 128:]


def live_parts(count, nb_ref):
    row = lax.broadcasted_iota(jnp.int32, (NEW * SLOTS_DEV, BOX), 0) & (SLOTS_DEV - 1)
    live = row < count
    return [
        jnp.where(live, nb_ref[q].reshape(NEW * SLOTS_DEV, BOX).astype(f32), 0.0).astype(bf16)
        for q in range(2)
    ]


def send_kernel(count_ref, nb_ref, res_ref, z_ref, out_ref, halves_ref):
    parts = live_parts(count_ref[0], nb_ref)
    acc = dot_nt(z_ref[0], parts[0]) + dot_nt(z_ref[1], parts[1])
    acc = acc[:384] + acc[384:]
    lane = lax.broadcasted_iota(jnp.int32, (COLUMNS, 128), 1) // 32
    for k in range(3):
        for group in range(GROUPS):
            total = jnp.zeros((COLUMNS, 128), f32)
            for c in range(4):
                piece = acc[(k * 4 + c) * 32 : (k * 4 + c + 1) * 32]
                shift = (c - group) * 32 % 128
                if shift:
                    piece = pltpu.roll(piece, shift, 1)
                total = jnp.where(lane == c, piece, total)
            out_ref[pl.ds(group * 128 + k, 32, stride=4), :] = total
    out_ref[pl.ds(3, 16, stride=4), :] = stick_sums(res_ref, parts, halves_ref)
    out_ref[pl.ds(67, 112, stride=4), :] = jnp.zeros((112, 128), f32)


def place_kernel(pos_ref, table_ref, pack_ref):
    pack_ref[TABLES:, :] = table_ref[...]
    pos = pos_ref[...].astype(f32)
    row = jnp.floor((pos + 0.5) * (1.0 / BOX))
    col = pos - row * BOX
    cell = jnp.floor(col * 0.5)
    side = (col - 2.0 * cell) * 128.0
    row = jnp.where(row < 48.0, row, row - 96.0)
    half = jnp.floor(row * 0.5)
    row = half + (row - 2.0 * half) * 48.0
    third = jnp.floor((cell + 0.5) * (1.0 / 32.0))
    lane_of = side + jnp.where(row < 72.0, cell, 96.0 + cell - 32.0 * third)
    row = jnp.transpose(jnp.where(row < 72.0, row, row - 72.0 + 24.0 * third))
    lane = lax.broadcasted_iota(jnp.int32, (DEVICES, 256), 1).astype(f32)
    index = lax.broadcasted_iota(jnp.int32, (2 * ROWS, 128), 0)
    index = jnp.where(index < ROWS, index, index - ROWS).astype(f32)
    for slot in range(SLOTS_DEV):
        hit = lane_of[:, slot : slot + 1] == lane
        pack_ref[slot * 128 : (slot + 1) * 128, :] = jnp.where(hit, 1.0, 0.0).astype(bf16)
        hit = jnp.broadcast_to(row[slot : slot + 1, :], (2 * ROWS, 128)) == index
        start = MASK + slot // 2 * 2 * ROWS
        lanes = slice(slot % 2 * 128, slot % 2 * 128 + 128)
        pack_ref[start : start + 2 * ROWS, lanes] = jnp.where(hit, 1.0, 0.0).astype(bf16)


def unfold(block):
    lane = lax.broadcasted_iota(jnp.int32, (24, 128), 1)
    last = pltpu.roll(block[48:72], 96, 1)
    last = jnp.where(lane < 64, pltpu.roll(block[24:48], 64, 1), last)
    last = jnp.where(lane < 32, pltpu.roll(block[:24], 32, 1), last)
    return jnp.concatenate([block, last], axis=0)


def fold(block):
    lane = lax.broadcasted_iota(jnp.int32, (24, 128), 1)
    thirds = [
        jnp.where(lane < 96, block[i * 24 : i * 24 + 24], pltpu.roll(block[72:96], 96 - 32 * i, 1))
        for i in range(3)
    ]
    return jnp.concatenate(thirds, axis=0)


CHUNK = 12


def box_kernel(
    in_ref, pot_any, pack_ref, out_ref, flat, high_v, low_v, grid, mid_h, mid_l, back, picked, pot_ref, sem
):
    move = pltpu.make_async_copy(pot_any, pot_ref, sem)
    move.start()

    def y_table(odd, part):
        start = TABLES + (odd * 2 + part) * 256
        return pack_ref[start : start + 256, :]

    def from_x(odd, rows):
        start = TABLES + 1792 + odd * 192
        return pack_ref[start : start + rows, :BOX]

    for k in range(3):
        flat[k * 128 : (k + 1) * 128, :] = jnp.transpose(in_ref[pl.ds(k, 128, stride=4), :])
    for slot in range(SLOTS_DEV):
        lanes = slice(slot * 128, (slot + 1) * 128)
        values = flat[pl.ds(slot, 24, stride=16), :]
        high = values.astype(bf16).astype(f32)
        high_v[:, lanes] = high
        low_v[:, lanes] = values - high

    def scatter(chunk, carry):
        mask = jnp.concatenate(
            [pack_ref[MASK + i * 2 * ROWS : MASK + (i + 1) * 2 * ROWS, :] for i in range(8)], axis=1
        )
        start = pl.multiple_of(chunk * (CHUNK * 96), 16)
        for part, source in enumerate((high_v, low_v)):
            blocks = []
            for i in range(0, CHUNK, 2):
                first = jnp.broadcast_to(source[pl.ds(chunk * CHUNK + i, 1), :], (8, 2048))
                second = jnp.broadcast_to(source[pl.ds(chunk * CHUNK + i + 1, 1), :], (8, 2048))
                upper = jnp.concatenate([first, first], axis=0).astype(bf16)
                middle = jnp.concatenate([first, second], axis=0).astype(bf16)
                lower = jnp.concatenate([second, second], axis=0).astype(bf16)
                blocks.append(mask * jnp.concatenate([upper] * 4 + [middle] + [lower] * 4, axis=0))
            term = dot(jnp.concatenate(blocks, axis=0), pack_ref[0:MASK, :])
            for odd in range(2):
                for i in range(CHUNK):
                    block = unfold(term[i * ROWS : (i + 1) * ROWS, odd * 128 : odd * 128 + 128])
                    grid[part, odd, pl.ds(start + i * 96, 96), :] = block.astype(bf16)
        return carry

    lax.fori_loop(0, 24 // CHUNK, scatter, 0)

    for part in range(3):
        outs = []
        for odd in range(2):
            high, low = [
                jnp.concatenate(
                    [grid[i, odd, base + part * 384 : base + part * 384 + 384, :] for base in (0, 1152)], axis=1
                )
                for i in range(2)
            ]
            outs.append(dot(high, y_table(odd, 0)) + dot(low, y_table(odd, 0)) + dot(high, y_table(odd, 1)))
        plus, minus = outs[0] + outs[1], outs[0] - outs[1]
        for q in range(2):
            lanes = slice(q * 128, q * 128 + 128)
            high, low = split(jnp.concatenate([plus[:, lanes], minus[:, lanes]], axis=1))
            for i in range(4):
                for half in range(2):
                    block = (slice(i * 96, i * 96 + 96), slice(half * 128, half * 128 + 128))
                    mid_h[part * 4 + i, half, q * 96 : q * 96 + 96, :] = high[block]
                    mid_l[part * 4 + i, half, q * 96 : q * 96 + 96, :] = low[block]

    move.wait()

    def one_plane(i, weight):
        high = jnp.concatenate([mid_h[i, 0], mid_h[i, 1]], axis=1)
        low = jnp.concatenate([mid_l[i, 0], mid_l[i, 1]], axis=1)
        field = dot(pack_ref[TABLES + 1024 : TABLES + 1792, :BOX], high)
        field = field[:384] + field[384:] + dot(pack_ref[TABLES + 1024 : TABLES + 1408, :BOX], low)
        re, im = field[:192] * weight, field[192:] * weight
        for odd in range(2):
            if odd:
                folded = jnp.concatenate([re[:96] - re[96:], im[:96] - im[96:]], axis=0)
            else:
                folded = jnp.concatenate([re[:96] + re[96:], im[:96] + im[96:]], axis=0)
            high, low = split(folded)
            out = dot(from_x(odd, 192), high)
            out = out[:96] + out[96:] + dot(from_x(odd, 96), low)
            start = pl.multiple_of(i * 96 + odd * 48, 8)
            back[pl.ds(start, 48), :] = out[:48]
            back[pl.ds(start + 1152, 48), :] = out[48:]

    def plane(p, carry):
        value = pot_ref[p]
        gap = jnp.zeros((BOX, 32), f32)
        weight = jnp.concatenate([value[:, :HALF], gap, value[:, HALF:], gap], axis=1)
        for i in range(2):
            one_plane(2 * p + i, weight)
        return carry

    lax.fori_loop(0, PLANES, plane, 0, unroll=2)

    for part in range(4):
        re = back[part * 288 : part * 288 + 288, :]
        im = back[1152 + part * 288 : 1152 + part * 288 + 288, :]
        outs = []
        for odd in range(2):
            if odd:
                pair = [re[:, :128] - re[:, 128:], im[:, :128] - im[:, 128:]]
            else:
                pair = [re[:, :128] + re[:, 128:], im[:, :128] + im[:, 128:]]
            high, low = split(jnp.concatenate(pair, axis=1))
            outs.append(
                dot_nt(high, y_table(odd, 0)) + dot_nt(low, y_table(odd, 0)) + dot_nt(high, y_table(odd, 1))
            )
        for q in range(2):
            lanes = slice(q * 128, q * 128 + 128)
            start = q * 12 * ROWS + part * 3 * ROWS
            for odd in range(2):
                rows = [fold(outs[odd][i * 96 : i * 96 + 96, lanes]) for i in range(3)]
                high, low = split(jnp.concatenate(rows, axis=0))
                picked[odd, start : start + 3 * ROWS, :] = high
                picked[2 + odd, start : start + 3 * ROWS, :] = low

    def pick(tile, carry):
        start = pl.multiple_of(tile * 256, 256)
        sel = pack_ref[pl.ds(start, 256), :]
        mask = pack_ref[pl.ds(pl.multiple_of(MASK + tile * 2 * ROWS, 16), 2 * ROWS), :].astype(f32)[:ROWS]
        size = 12 * ROWS
        totals = []
        for i in range(4):
            part = i // 2 * 2
            rows = slice(i % 2 * size, i % 2 * size + size)
            out = dot_nt(jnp.concatenate([picked[part, rows], picked[part + 1, rows]], axis=1), sel)
            totals.append(jnp.sum(out.reshape(12, ROWS, 256) * mask[None], axis=1))
        total = jnp.concatenate([totals[0] + totals[2], totals[1] + totals[3]], axis=0)
        flat[pl.ds(2 * tile, 24, stride=16), :] = total[:, :128]
        flat[pl.ds(2 * tile + 1, 24, stride=16), :] = total[:, 128:]
        return carry

    lax.fori_loop(0, 8, pick, 0, unroll=4)

    for k in range(3):
        out_ref[pl.ds(k, 128, stride=4), :] = jnp.transpose(flat[k * 128 : (k + 1) * 128, :])
    total = jnp.sum(in_ref[pl.ds(3, 128, stride=4), :], axis=0, keepdims=True)
    out_ref[pl.ds(3, 128, stride=4), :] = jnp.broadcast_to(total, (DEVICES, 128))


def apply_kernel(
    count_ref, pos_ref, in_ref, nb_ref, res_ref, z_ref, applied_ref, keep_ref, give_ref, inter_ref,
    halves_ref,
):
    device = lax.axis_index("band") * COLUMNS + lax.axis_index("fft")
    lane = lax.broadcasted_iota(jnp.int32, (COLUMNS, 128), 1) // 32
    pieces = []
    for k in range(3):
        for c in range(4):
            total = jnp.zeros((COLUMNS, 128), f32)
            for group in range(GROUPS):
                piece = in_ref[pl.ds(group * 128 + k, 32, stride=4), :]
                shift = (group - c) * 32 % 128
                if shift:
                    piece = pltpu.roll(piece, shift, 1)
                total = jnp.where(lane == group, piece, total)
            pieces.append(total)
    field = jnp.transpose(jnp.concatenate(pieces, axis=0))
    high, low = split(field)
    parts = live_parts(count_ref[0], nb_ref)
    row = lax.broadcasted_iota(jnp.int32, (NEW * SLOTS_DEV, BOX), 0) & (SLOTS_DEV - 1)
    squares = jnp.zeros((NEW * SLOTS_DEV, BOX), f32)
    for slot in range(SLOTS_DEV):
        pos = pos_ref[device * SLOTS_DEV + slot]
        kx = lax.div(pos, jnp.int32(BOX))
        ky = pos - kx * BOX
        kx = jnp.where(kx < HALF, kx, kx - BOX)
        ky = jnp.where(ky < HALF, ky, ky - BOX)
        squares = jnp.where(row == slot, (kx * kx + ky * ky).astype(f32), squares)
    kz = lax.broadcasted_iota(jnp.int32, (NEW * SLOTS_DEV, BOX), 1)
    kz = jnp.where(kz < HALF, kz, kz - BOX).astype(f32)
    kinetic = 2.0 * (squares + kz * kz) / float(BOX * BOX)
    live = row < count_ref[0]
    applied = []
    for q in range(2):
        table = z_ref[q]
        spectrum = dot(high, table[:384]) + dot(low, table[:384]) + dot(high, table[384:])
        spectrum = spectrum * (1.0 / BOX**3)
        value = jnp.where(live, kinetic * parts[q].astype(f32) + spectrum, 0.0).astype(bf16)
        applied.append(value)
        applied_ref[q] = value.reshape(NEW, SLOTS_DEV, BOX)
    sums = stick_sums(res_ref, applied, halves_ref)
    first = lax.rem(device, 2) == 0
    keep_ref[...] = jnp.where(first, sums[:8], sums[8:])
    give_ref[...] = jnp.where(first, sums[8:], sums[:8])
    inter_ref[...] = in_ref[pl.ds(3, 16, stride=4), :].reshape(2, NEW, RES)


def pair_kernel(keep_ref, came_ref, out_ref):
    total = keep_ref[...] + came_ref[...]
    out_ref[...] = jnp.broadcast_to(total[None], (DEVICES // 2, 8, 128)).reshape(512, 128)


def sum_kernel(in_ref, out_ref):
    total = in_ref[0:8, :]
    for i in range(8, 512, 8):
        total = total + in_ref[i : i + 8, :]
    out_ref[...] = total


def join_kernel(mine_ref, other_ref, out_ref):
    first = lax.rem(lax.axis_index("fft"), 2) == 0
    mine, other = mine_ref[...], other_ref[...]
    low = jnp.where(first, mine, other)
    high = jnp.where(first, other, mine)
    for q in range(2):
        rows = slice(q * 4, q * 4 + 4)
        out_ref[q] = jnp.concatenate([low[rows], high[rows]], axis=0)


WHOLE = 60000 * 1024
vmem = pl.BlockSpec(memory_space=pltpu.VMEM)
smem = pl.BlockSpec(memory_space=pltpu.SMEM)


def call(body, out_shape, in_specs, name, scratch=(), limit=24 << 20):
    return pl.pallas_call(
        body,
        out_shape=out_shape,
        in_specs=in_specs,
        out_specs=jax.tree.map(lambda _: vmem, out_shape),
        scratch_shapes=list(scratch),
        name=name,
        compiler_params=pltpu.CompilerParams(vmem_limit_bytes=limit),
        cost_estimate=pl.CostEstimate(flops=0, bytes_accessed=1 << 20, transcendentals=0),
    )


def shaped(shape, dtype=f32):
    return jax.ShapeDtypeStruct(shape, dtype)


def exchange(values, rows):
    values = values.reshape(DEVICES, rows, 128)
    return lax.all_to_all(values, both, split_axis=0, concat_axis=0, tiled=True)


def local(tables, new_bands, resident, potential, stick_pos, stick_count):
    z_table, box_tables = [jnp.asarray(table) for table in tables]
    resident = jnp.transpose(resident, (0, 2, 3, 1))
    halves_shape = pltpu.VMEM((2, 2, 128, 128), f32)
    sent = call(
        send_kernel, shaped((512, 128)), [smem, vmem, vmem, vmem], "send", scratch=[halves_shape], limit=WHOLE
    )(stick_count, new_bands, resident, z_table)
    came = exchange(sent, 4).reshape(512, 128)
    pack = call(
        place_kernel,
        shaped((TABLES + 2176, 256), bf16),
        [vmem] * 2,
        "place",
        limit=16 << 20,
    )(stick_pos.reshape(DEVICES, SLOTS_DEV), box_tables)
    result = call(
        box_kernel,
        shaped((512, 128)),
        [vmem, pl.BlockSpec(memory_space=pltpu.HBM), vmem],
        "box",
        scratch=[
            pltpu.VMEM((384, 128), f32),
            pltpu.VMEM((24, 2048), f32),
            pltpu.VMEM((24, 2048), f32),
            pltpu.VMEM((2, 2, 2304, 128), bf16),
            pltpu.VMEM((12, 2, 192, 128), bf16),
            pltpu.VMEM((12, 2, 192, 128), bf16),
            pltpu.VMEM((2304, 256), f32),
            pltpu.VMEM((4, 24 * ROWS, 128), bf16),
            pltpu.VMEM((PLANES, BOX, BOX), f32),
            pltpu.SemaphoreType.DMA,
        ],
        limit=40 << 20,
    )(came, pltpu.with_memory_space_constraint(potential, pltpu.HBM), pack)
    returned = exchange(result, 4).reshape(512, 128)
    applied, keep, give, inter = call(
        apply_kernel,
        (
            shaped((2, NEW, SLOTS_DEV, BOX), bf16),
            shaped((8, 128)),
            shaped((8, 128)),
            shaped((2, NEW, RES)),
        ),
        [smem, smem, vmem, vmem, vmem, vmem],
        "apply",
        scratch=[halves_shape],
    )(stick_count, stick_pos, returned, new_bands, resident, z_table)
    pairs = [(i, i ^ 1) for i in range(COLUMNS)]
    other = lax.ppermute(give, "fft", pairs)
    partial = call(pair_kernel, shaped((512, 128)), [vmem, vmem], "pair")(keep, other)
    mine = call(sum_kernel, shaped((8, 128)), [vmem], "total")(exchange(partial, 4).reshape(512, 128))
    other = lax.ppermute(mine, "fft", pairs)
    proj = call(join_kernel, shaped((2, NEW, RES)), [vmem, vmem], "join")(mine, other)
    return applied, jnp.transpose(proj, (0, 2, 1)), jnp.transpose(inter, (0, 2, 1))


def solution(mesh):
    return jax.shard_map(
        functools.partial(local, make_tables()),
        mesh=mesh,
        in_specs=(
            P(None, None, both, None),
            P(None, None, both, None),
            P("fft", None, None),
            P(),
            P(both),
        ),
        out_specs=(P(None, None, both, None), P(), P()),
        check_vma=False,
    )
```

```python
import functools

import jax
import jax.numpy as jnp
import ml_dtypes
import numpy as np
from jax import lax
from jax.experimental import pallas as pl
from jax.experimental.pallas import tpu as pltpu
from jax.sharding import PartitionSpec as P

BOX = 192
HALF = 96
SLOTS_DEV = 16
NEW = 8
RES = 128
DEVICES = 128
PLANES = 6
GROUPS = 4
COLUMNS = 32
ROWS = 72
f32 = jnp.float32
bf16 = jnp.bfloat16
both = ("band", "fft")
MASK = 2048
TABLES = MASK + 8 * 2 * ROWS


def halves(table):
    high = table.astype(ml_dtypes.bfloat16)
    low = (table - high.astype(np.float64)).astype(ml_dtypes.bfloat16)
    return high, low


def wave(rows, cols):
    return 2.0 * np.pi / BOX * ((rows[:, None] * cols[None, :]) % BOX)


def rotation(angles):
    return [[np.cos(angles), -np.sin(angles)], [np.sin(angles), np.cos(angles)]]


def make_tables():
    plane = (np.arange(COLUMNS)[None, :] * PLANES + np.arange(PLANES)[:, None]).reshape(-1)
    blocks = rotation(wave(plane, np.arange(BOX)))
    z_table = []
    for q in range(2):
        high, low = halves(np.concatenate([blocks[0][q], blocks[1][q]], axis=0))
        z_table.append(np.concatenate([high, low], axis=0))
    z_table = np.stack(z_table)
    y_table = []
    for odd in range(2):
        blocks = rotation(wave(2 * np.arange(HALF) + odd, np.arange(HALF)))
        full = np.zeros((2, 128, 2, 128))
        for q_in in range(2):
            for q_out in range(2):
                full[q_in, :HALF, q_out, :HALF] = blocks[q_out][q_in]
        y_table.append(np.stack(halves(full.reshape(256, 256))))
    y_table = np.stack(y_table)
    index = np.concatenate([2 * np.arange(48), 2 * np.arange(48) + 1])
    freq = np.where(index < 48, index, index + 96)
    blocks = rotation(wave(np.arange(BOX), freq))
    to_x = np.block(blocks)
    to_x = np.stack(halves(to_x))
    from_x = []
    for odd in range(2):
        angles = -wave(freq[odd * 48 : odd * 48 + 48], np.arange(HALF))
        from_x.append(np.stack(halves(np.block(rotation(angles)))))
    wide = np.concatenate([to_x.reshape(768, BOX), np.stack(from_x).reshape(384, BOX)])
    wide = np.concatenate([wide, np.zeros((1152, 64), wide.dtype)], axis=1)
    return z_table, np.concatenate([y_table.reshape(1024, 256), wide])


def dot(a, b):
    return lax.dot_general(a, b, (((1,), (0,)), ((), ())), preferred_element_type=f32)


def dot_nt(a, b):
    return lax.dot_general(a, b, (((1,), (1,)), ((), ())), preferred_element_type=f32)


def split(values):
    high = values.astype(bf16)
    return high, (values - high.astype(f32)).astype(bf16)


def stick_sums(res_ref, parts, halves_ref):
    for q in range(2):
        halves_ref[q, 0] = parts[q][:, :128].astype(f32)
        halves_ref[q, 1, :, 0:64] = parts[q][:, 128:].astype(f32)
    totals = [jnp.zeros((32, 256), f32)] * 2
    for slot in range(SLOTS_DEV):
        v0, v1 = [
            jnp.concatenate(
                [halves_ref[q, half, pl.ds(slot, 8, stride=16), :][:, :width] for half, width in ((0, 128), (1, 64))],
                axis=1,
            )
            for q in range(2)
        ]
        left = jnp.concatenate([v0, v1, v1, -v0], axis=0).astype(bf16)
        right = jnp.concatenate([res_ref[0, slot], res_ref[1, slot]], axis=1)
        totals[slot % 2] = totals[slot % 2] + dot(left, right)
    total = sum(totals[1:], totals[0])
    return total[:16, :128] + total[16:, 128:]


def live_parts(count, nb_ref):
    row = lax.broadcasted_iota(jnp.int32, (NEW * SLOTS_DEV, BOX), 0) & (SLOTS_DEV - 1)
    live = row < count
    return [
        jnp.where(live, nb_ref[q].reshape(NEW * SLOTS_DEV, BOX).astype(f32), 0.0).astype(bf16)
        for q in range(2)
    ]


def send_kernel(count_ref, nb_ref, res_ref, z_ref, out_ref, halves_ref):
    parts = live_parts(count_ref[0], nb_ref)
    acc = dot_nt(z_ref[0], parts[0]) + dot_nt(z_ref[1], parts[1])
    acc = acc[:384] + acc[384:]
    lane = lax.broadcasted_iota(jnp.int32, (COLUMNS, 128), 1) // 32
    for k in range(3):
        for group in range(GROUPS):
            total = jnp.zeros((COLUMNS, 128), f32)
            for c in range(4):
                piece = acc[(k * 4 + c) * 32 : (k * 4 + c + 1) * 32]
                shift = (c - group) * 32 % 128
                if shift:
                    piece = pltpu.roll(piece, shift, 1)
                total = jnp.where(lane == c, piece, total)
            out_ref[pl.ds(group * 128 + k, 32, stride=4), :] = total
    out_ref[pl.ds(3, 16, stride=4), :] = stick_sums(res_ref, parts, halves_ref)
    out_ref[pl.ds(67, 112, stride=4), :] = jnp.zeros((112, 128), f32)


def place_kernel(pos_ref, table_ref, pack_ref):
    pack_ref[TABLES:, :] = table_ref[...]
    pos = pos_ref[...].astype(f32)
    row = jnp.floor((pos + 0.5) * (1.0 / BOX))
    col = pos - row * BOX
    cell = jnp.floor(col * 0.5)
    side = (col - 2.0 * cell) * 128.0
    row = jnp.where(row < 48.0, row, row - 96.0)
    half = jnp.floor(row * 0.5)
    row = half + (row - 2.0 * half) * 48.0
    third = jnp.floor((cell + 0.5) * (1.0 / 32.0))
    lane_of = side + jnp.where(row < 72.0, cell, 96.0 + cell - 32.0 * third)
    row = jnp.transpose(jnp.where(row < 72.0, row, row - 72.0 + 24.0 * third))
    lane = lax.broadcasted_iota(jnp.int32, (DEVICES, 256), 1).astype(f32)
    index = lax.broadcasted_iota(jnp.int32, (2 * ROWS, 128), 0)
    index = jnp.where(index < ROWS, index, index - ROWS).astype(f32)
    for slot in range(SLOTS_DEV):
        hit = lane_of[:, slot : slot + 1] == lane
        pack_ref[slot * 128 : (slot + 1) * 128, :] = jnp.where(hit, 1.0, 0.0).astype(bf16)
        hit = jnp.broadcast_to(row[slot : slot + 1, :], (2 * ROWS, 128)) == index
        start = MASK + slot // 2 * 2 * ROWS
        lanes = slice(slot % 2 * 128, slot % 2 * 128 + 128)
        pack_ref[start : start + 2 * ROWS, lanes] = jnp.where(hit, 1.0, 0.0).astype(bf16)


def unfold(block):
    lane = lax.broadcasted_iota(jnp.int32, (24, 128), 1)
    last = pltpu.roll(block[48:72], 96, 1)
    last = jnp.where(lane < 64, pltpu.roll(block[24:48], 64, 1), last)
    last = jnp.where(lane < 32, pltpu.roll(block[:24], 32, 1), last)
    return jnp.concatenate([block, last], axis=0)


def fold(block):
    lane = lax.broadcasted_iota(jnp.int32, (24, 128), 1)
    thirds = [
        jnp.where(lane < 96, block[i * 24 : i * 24 + 24], pltpu.roll(block[72:96], 96 - 32 * i, 1))
        for i in range(3)
    ]
    return jnp.concatenate(thirds, axis=0)


CHUNK = 12


def box_kernel(
    in_ref, pot_any, pack_ref, out_ref, flat, high_v, low_v, grid, mid_h, mid_l, back, picked, pot_ref, sem
):
    move = pltpu.make_async_copy(pot_any, pot_ref, sem)
    move.start()

    def y_table(odd, part):
        start = TABLES + (odd * 2 + part) * 256
        return pack_ref[start : start + 256, :]

    def from_x(odd, rows):
        start = TABLES + 1792 + odd * 192
        return pack_ref[start : start + rows, :BOX]

    for k in range(3):
        flat[k * 128 : (k + 1) * 128, :] = jnp.transpose(in_ref[pl.ds(k, 128, stride=4), :])
    for slot in range(SLOTS_DEV):
        lanes = slice(slot * 128, (slot + 1) * 128)
        values = flat[pl.ds(slot, 24, stride=16), :]
        high = values.astype(bf16).astype(f32)
        high_v[:, lanes] = high
        low_v[:, lanes] = values - high

    def scatter(chunk, carry):
        mask = jnp.concatenate(
            [pack_ref[MASK + i * 2 * ROWS : MASK + (i + 1) * 2 * ROWS, :] for i in range(8)], axis=1
        )
        start = pl.multiple_of(chunk * (CHUNK * 96), 16)
        for part, source in enumerate((high_v, low_v)):
            blocks = []
            for i in range(0, CHUNK, 2):
                first = jnp.broadcast_to(source[pl.ds(chunk * CHUNK + i, 1), :], (8, 2048))
                second = jnp.broadcast_to(source[pl.ds(chunk * CHUNK + i + 1, 1), :], (8, 2048))
                upper = jnp.concatenate([first, first], axis=0).astype(bf16)
                middle = jnp.concatenate([first, second], axis=0).astype(bf16)
                lower = jnp.concatenate([second, second], axis=0).astype(bf16)
                blocks.append(mask * jnp.concatenate([upper] * 4 + [middle] + [lower] * 4, axis=0))
            term = dot(jnp.concatenate(blocks, axis=0), pack_ref[0:MASK, :])
            for odd in range(2):
                for i in range(CHUNK):
                    block = unfold(term[i * ROWS : (i + 1) * ROWS, odd * 128 : odd * 128 + 128])
                    grid[part, odd, pl.ds(start + i * 96, 96), :] = block.astype(bf16)
        return carry

    lax.fori_loop(0, 24 // CHUNK, scatter, 0)

    for part in range(3):
        outs = []
        for odd in range(2):
            high, low = [
                jnp.concatenate(
                    [grid[i, odd, base + part * 384 : base + part * 384 + 384, :] for base in (0, 1152)], axis=1
                )
                for i in range(2)
            ]
            outs.append(dot(high, y_table(odd, 0)) + dot(low, y_table(odd, 0)) + dot(high, y_table(odd, 1)))
        plus, minus = outs[0] + outs[1], outs[0] - outs[1]
        for q in range(2):
            lanes = slice(q * 128, q * 128 + 128)
            high, low = split(jnp.concatenate([plus[:, lanes], minus[:, lanes]], axis=1))
            for i in range(4):
                for half in range(2):
                    block = (slice(i * 96, i * 96 + 96), slice(half * 128, half * 128 + 128))
                    mid_h[part * 4 + i, half, q * 96 : q * 96 + 96, :] = high[block]
                    mid_l[part * 4 + i, half, q * 96 : q * 96 + 96, :] = low[block]

    move.wait()

    def one_plane(i, weight):
        high = jnp.concatenate([mid_h[i, 0], mid_h[i, 1]], axis=1)
        low = jnp.concatenate([mid_l[i, 0], mid_l[i, 1]], axis=1)
        field = dot(pack_ref[TABLES + 1024 : TABLES + 1792, :BOX], high)
        field = field[:384] + field[384:] + dot(pack_ref[TABLES + 1024 : TABLES + 1408, :BOX], low)
        re, im = field[:192] * weight, field[192:] * weight
        for odd in range(2):
            if odd:
                folded = jnp.concatenate([re[:96] - re[96:], im[:96] - im[96:]], axis=0)
            else:
                folded = jnp.concatenate([re[:96] + re[96:], im[:96] + im[96:]], axis=0)
            high, low = split(folded)
            out = dot(from_x(odd, 192), high)
            out = out[:96] + out[96:] + dot(from_x(odd, 96), low)
            start = pl.multiple_of(i * 96 + odd * 48, 8)
            back[pl.ds(start, 48), :] = out[:48]
            back[pl.ds(start + 1152, 48), :] = out[48:]

    def plane(p, carry):
        value = pot_ref[p]
        gap = jnp.zeros((BOX, 32), f32)
        weight = jnp.concatenate([value[:, :HALF], gap, value[:, HALF:], gap], axis=1)
        for i in range(2):
            one_plane(2 * p + i, weight)
        return carry

    lax.fori_loop(0, PLANES, plane, 0, unroll=3)

    for part in range(4):
        re = back[part * 288 : part * 288 + 288, :]
        im = back[1152 + part * 288 : 1152 + part * 288 + 288, :]
        outs = []
        for odd in range(2):
            if odd:
                pair = [re[:, :128] - re[:, 128:], im[:, :128] - im[:, 128:]]
            else:
                pair = [re[:, :128] + re[:, 128:], im[:, :128] + im[:, 128:]]
            high, low = split(jnp.concatenate(pair, axis=1))
            outs.append(
                dot_nt(high, y_table(odd, 0)) + dot_nt(low, y_table(odd, 0)) + dot_nt(high, y_table(odd, 1))
            )
        for q in range(2):
            lanes = slice(q * 128, q * 128 + 128)
            start = q * 12 * ROWS + part * 3 * ROWS
            for odd in range(2):
                rows = [fold(outs[odd][i * 96 : i * 96 + 96, lanes]) for i in range(3)]
                high, low = split(jnp.concatenate(rows, axis=0))
                picked[odd, start : start + 3 * ROWS, :] = high
                picked[2 + odd, start : start + 3 * ROWS, :] = low

    def pick(tile, carry):
        start = pl.multiple_of(tile * 256, 256)
        sel = pack_ref[pl.ds(start, 256), :]
        mask = pack_ref[pl.ds(pl.multiple_of(MASK + tile * 2 * ROWS, 16), 2 * ROWS), :].astype(f32)[:ROWS]
        size = 12 * ROWS
        totals = []
        for i in range(4):
            part = i // 2 * 2
            rows = slice(i % 2 * size, i % 2 * size + size)
            out = dot_nt(jnp.concatenate([picked[part, rows], picked[part + 1, rows]], axis=1), sel)
            totals.append(jnp.sum(out.reshape(12, ROWS, 256) * mask[None], axis=1))
        total = jnp.concatenate([totals[0] + totals[2], totals[1] + totals[3]], axis=0)
        flat[pl.ds(2 * tile, 24, stride=16), :] = total[:, :128]
        flat[pl.ds(2 * tile + 1, 24, stride=16), :] = total[:, 128:]
        return carry

    lax.fori_loop(0, 8, pick, 0, unroll=4)

    for k in range(3):
        out_ref[pl.ds(k, 128, stride=4), :] = jnp.transpose(flat[k * 128 : (k + 1) * 128, :])
    total = jnp.sum(in_ref[pl.ds(3, 128, stride=4), :], axis=0, keepdims=True)
    out_ref[pl.ds(3, 128, stride=4), :] = jnp.broadcast_to(total, (DEVICES, 128))


def apply_kernel(
    count_ref, pos_ref, in_ref, nb_ref, res_ref, z_ref, applied_ref, keep_ref, give_ref, inter_ref,
    halves_ref,
):
    device = lax.axis_index("band") * COLUMNS + lax.axis_index("fft")
    lane = lax.broadcasted_iota(jnp.int32, (COLUMNS, 128), 1) // 32
    pieces = []
    for k in range(3):
        for c in range(4):
            total = jnp.zeros((COLUMNS, 128), f32)
            for group in range(GROUPS):
                piece = in_ref[pl.ds(group * 128 + k, 32, stride=4), :]
                shift = (group - c) * 32 % 128
                if shift:
                    piece = pltpu.roll(piece, shift, 1)
                total = jnp.where(lane == group, piece, total)
            pieces.append(total)
    field = jnp.transpose(jnp.concatenate(pieces, axis=0))
    high, low = split(field)
    parts = live_parts(count_ref[0], nb_ref)
    row = lax.broadcasted_iota(jnp.int32, (NEW * SLOTS_DEV, BOX), 0) & (SLOTS_DEV - 1)
    squares = jnp.zeros((NEW * SLOTS_DEV, BOX), f32)
    for slot in range(SLOTS_DEV):
        pos = pos_ref[device * SLOTS_DEV + slot]
        kx = lax.div(pos, jnp.int32(BOX))
        ky = pos - kx * BOX
        kx = jnp.where(kx < HALF, kx, kx - BOX)
        ky = jnp.where(ky < HALF, ky, ky - BOX)
        squares = jnp.where(row == slot, (kx * kx + ky * ky).astype(f32), squares)
    kz = lax.broadcasted_iota(jnp.int32, (NEW * SLOTS_DEV, BOX), 1)
    kz = jnp.where(kz < HALF, kz, kz - BOX).astype(f32)
    kinetic = 2.0 * (squares + kz * kz) / float(BOX * BOX)
    live = row < count_ref[0]
    applied = []
    for q in range(2):
        table = z_ref[q]
        spectrum = dot(high, table[:384]) + dot(low, table[:384]) + dot(high, table[384:])
        spectrum = spectrum * (1.0 / BOX**3)
        value = jnp.where(live, kinetic * parts[q].astype(f32) + spectrum, 0.0).astype(bf16)
        applied.append(value)
        applied_ref[q] = value.reshape(NEW, SLOTS_DEV, BOX)
    sums = stick_sums(res_ref, applied, halves_ref)
    first = lax.rem(device, 2) == 0
    keep_ref[...] = jnp.where(first, sums[:8], sums[8:])
    give_ref[...] = jnp.where(first, sums[8:], sums[:8])
    inter_ref[...] = in_ref[pl.ds(3, 16, stride=4), :].reshape(2, NEW, RES)


def pair_kernel(keep_ref, came_ref, out_ref):
    total = keep_ref[...] + came_ref[...]
    out_ref[...] = jnp.broadcast_to(total[None], (DEVICES // 2, 8, 128)).reshape(512, 128)


def sum_kernel(in_ref, out_ref):
    total = in_ref[0:8, :]
    for i in range(8, 512, 8):
        total = total + in_ref[i : i + 8, :]
    out_ref[...] = total


def join_kernel(mine_ref, other_ref, out_ref):
    first = lax.rem(lax.axis_index("fft"), 2) == 0
    mine, other = mine_ref[...], other_ref[...]
    low = jnp.where(first, mine, other)
    high = jnp.where(first, other, mine)
    for q in range(2):
        rows = slice(q * 4, q * 4 + 4)
        out_ref[q] = jnp.concatenate([low[rows], high[rows]], axis=0)


WHOLE = 60000 * 1024
vmem = pl.BlockSpec(memory_space=pltpu.VMEM)
smem = pl.BlockSpec(memory_space=pltpu.SMEM)


def call(body, out_shape, in_specs, name, scratch=(), limit=24 << 20):
    return pl.pallas_call(
        body,
        out_shape=out_shape,
        in_specs=in_specs,
        out_specs=jax.tree.map(lambda _: vmem, out_shape),
        scratch_shapes=list(scratch),
        name=name,
        compiler_params=pltpu.CompilerParams(vmem_limit_bytes=limit),
        cost_estimate=pl.CostEstimate(flops=0, bytes_accessed=1 << 20, transcendentals=0),
    )


def shaped(shape, dtype=f32):
    return jax.ShapeDtypeStruct(shape, dtype)


def exchange(values, rows):
    values = values.reshape(DEVICES, rows, 128)
    return lax.all_to_all(values, both, split_axis=0, concat_axis=0, tiled=True)


def local(tables, new_bands, resident, potential, stick_pos, stick_count):
    z_table, box_tables = [jnp.asarray(table) for table in tables]
    resident = jnp.transpose(resident, (0, 2, 3, 1))
    halves_shape = pltpu.VMEM((2, 2, 128, 128), f32)
    sent = call(
        send_kernel, shaped((512, 128)), [smem, vmem, vmem, vmem], "send", scratch=[halves_shape], limit=WHOLE
    )(stick_count, new_bands, resident, z_table)
    came = exchange(sent, 4).reshape(512, 128)
    pack = call(
        place_kernel,
        shaped((TABLES + 2176, 256), bf16),
        [vmem] * 2,
        "place",
        limit=16 << 20,
    )(stick_pos.reshape(DEVICES, SLOTS_DEV), box_tables)
    result = call(
        box_kernel,
        shaped((512, 128)),
        [vmem, pl.BlockSpec(memory_space=pltpu.HBM), vmem],
        "box",
        scratch=[
            pltpu.VMEM((384, 128), f32),
            pltpu.VMEM((24, 2048), f32),
            pltpu.VMEM((24, 2048), f32),
            pltpu.VMEM((2, 2, 2304, 128), bf16),
            pltpu.VMEM((12, 2, 192, 128), bf16),
            pltpu.VMEM((12, 2, 192, 128), bf16),
            pltpu.VMEM((2304, 256), f32),
            pltpu.VMEM((4, 24 * ROWS, 128), bf16),
            pltpu.VMEM((PLANES, BOX, BOX), f32),
            pltpu.SemaphoreType.DMA,
        ],
        limit=40 << 20,
    )(came, pltpu.with_memory_space_constraint(potential, pltpu.HBM), pack)
    returned = exchange(result, 4).reshape(512, 128)
    applied, keep, give, inter = call(
        apply_kernel,
        (
            shaped((2, NEW, SLOTS_DEV, BOX), bf16),
            shaped((8, 128)),
            shaped((8, 128)),
            shaped((2, NEW, RES)),
        ),
        [smem, smem, vmem, vmem, vmem, vmem],
        "apply",
        scratch=[halves_shape],
    )(stick_count, stick_pos, returned, new_bands, resident, z_table)
    pairs = [(i, i ^ 1) for i in range(COLUMNS)]
    other = lax.ppermute(give, "fft", pairs)
    partial = call(pair_kernel, shaped((512, 128)), [vmem, vmem], "pair")(keep, other)
    mine = call(sum_kernel, shaped((8, 128)), [vmem], "total")(exchange(partial, 4).reshape(512, 128))
    other = lax.ppermute(mine, "fft", pairs)
    proj = call(join_kernel, shaped((2, NEW, RES)), [vmem, vmem], "join")(mine, other)
    return applied, jnp.transpose(proj, (0, 2, 1)), jnp.transpose(inter, (0, 2, 1))


def solution(mesh):
    return jax.shard_map(
        functools.partial(local, make_tables()),
        mesh=mesh,
        in_specs=(
            P(None, None, both, None),
            P(None, None, both, None),
            P("fft", None, None),
            P(),
            P(both),
        ),
        out_specs=(P(None, None, both, None), P(), P()),
        check_vma=False,
    )
```

```python
import functools

import jax
import jax.numpy as jnp
import ml_dtypes
import numpy as np
from jax import lax
from jax.experimental import pallas as pl
from jax.experimental.pallas import tpu as pltpu
from jax.sharding import PartitionSpec as P

BOX = 192
HALF = 96
SLOTS_DEV = 16
NEW = 8
RES = 128
DEVICES = 128
PLANES = 6
GROUPS = 4
COLUMNS = 32
ROWS = 72
f32 = jnp.float32
bf16 = jnp.bfloat16
both = ("band", "fft")
MASK = 2048
TABLES = MASK + 8 * 2 * ROWS


def halves(table):
    high = table.astype(ml_dtypes.bfloat16)
    low = (table - high.astype(np.float64)).astype(ml_dtypes.bfloat16)
    return high, low


def wave(rows, cols):
    return 2.0 * np.pi / BOX * ((rows[:, None] * cols[None, :]) % BOX)


def rotation(angles):
    return [[np.cos(angles), -np.sin(angles)], [np.sin(angles), np.cos(angles)]]


def make_tables():
    plane = (np.arange(COLUMNS)[None, :] * PLANES + np.arange(PLANES)[:, None]).reshape(-1)
    blocks = rotation(wave(plane, np.arange(BOX)))
    z_table = []
    for q in range(2):
        high, low = halves(np.concatenate([blocks[0][q], blocks[1][q]], axis=0))
        z_table.append(np.concatenate([high, low], axis=0))
    z_table = np.stack(z_table)
    y_table = []
    for odd in range(2):
        blocks = rotation(wave(2 * np.arange(HALF) + odd, np.arange(HALF)))
        full = np.zeros((2, 128, 2, 128))
        for q_in in range(2):
            for q_out in range(2):
                full[q_in, :HALF, q_out, :HALF] = blocks[q_out][q_in]
        y_table.append(np.stack(halves(full.reshape(256, 256))))
    y_table = np.stack(y_table)
    index = np.concatenate([2 * np.arange(48), 2 * np.arange(48) + 1])
    freq = np.where(index < 48, index, index + 96)
    blocks = rotation(wave(np.arange(BOX), freq))
    to_x = np.block(blocks)
    to_x = np.stack(halves(to_x))
    from_x = []
    for odd in range(2):
        angles = -wave(freq[odd * 48 : odd * 48 + 48], np.arange(HALF))
        from_x.append(np.stack(halves(np.block(rotation(angles)))))
    wide = np.concatenate([to_x.reshape(768, BOX), np.stack(from_x).reshape(384, BOX)])
    wide = np.concatenate([wide, np.zeros((1152, 64), wide.dtype)], axis=1)
    return z_table, np.concatenate([y_table.reshape(1024, 256), wide])


def dot(a, b):
    return lax.dot_general(a, b, (((1,), (0,)), ((), ())), preferred_element_type=f32)


def dot_nt(a, b):
    return lax.dot_general(a, b, (((1,), (1,)), ((), ())), preferred_element_type=f32)


def split(values):
    high = values.astype(bf16)
    return high, (values - high.astype(f32)).astype(bf16)


def stick_sums(res_ref, parts, halves_ref):
    for q in range(2):
        halves_ref[q, 0] = parts[q][:, :128].astype(f32)
        halves_ref[q, 1, :, 0:64] = parts[q][:, 128:].astype(f32)
    totals = [jnp.zeros((32, 256), f32)] * 2
    for slot in range(SLOTS_DEV):
        v0, v1 = [
            jnp.concatenate(
                [halves_ref[q, half, pl.ds(slot, 8, stride=16), :][:, :width] for half, width in ((0, 128), (1, 64))],
                axis=1,
            )
            for q in range(2)
        ]
        left = jnp.concatenate([v0, v1, v1, -v0], axis=0).astype(bf16)
        right = jnp.concatenate([res_ref[0, slot], res_ref[1, slot]], axis=1)
        totals[slot % 2] = totals[slot % 2] + dot(left, right)
    total = sum(totals[1:], totals[0])
    return total[:16, :128] + total[16:, 128:]


def live_parts(count, nb_ref):
    row = lax.broadcasted_iota(jnp.int32, (NEW * SLOTS_DEV, BOX), 0) & (SLOTS_DEV - 1)
    live = row < count
    return [
        jnp.where(live, nb_ref[q].reshape(NEW * SLOTS_DEV, BOX).astype(f32), 0.0).astype(bf16)
        for q in range(2)
    ]


def send_kernel(count_ref, nb_ref, res_ref, z_ref, out_ref, halves_ref):
    parts = live_parts(count_ref[0], nb_ref)
    acc = dot_nt(z_ref[0], parts[0]) + dot_nt(z_ref[1], parts[1])
    acc = acc[:384] + acc[384:]
    lane = lax.broadcasted_iota(jnp.int32, (COLUMNS, 128), 1) // 32
    for k in range(3):
        for group in range(GROUPS):
            total = jnp.zeros((COLUMNS, 128), f32)
            for c in range(4):
                piece = acc[(k * 4 + c) * 32 : (k * 4 + c + 1) * 32]
                shift = (c - group) * 32 % 128
                if shift:
                    piece = pltpu.roll(piece, shift, 1)
                total = jnp.where(lane == c, piece, total)
            out_ref[pl.ds(group * 128 + k, 32, stride=4), :] = total
    out_ref[pl.ds(3, 16, stride=4), :] = stick_sums(res_ref, parts, halves_ref)
    out_ref[pl.ds(67, 112, stride=4), :] = jnp.zeros((112, 128), f32)


def place_kernel(pos_ref, table_ref, pack_ref):
    pack_ref[TABLES:, :] = table_ref[...]
    pos = pos_ref[...].astype(f32)
    row = jnp.floor((pos + 0.5) * (1.0 / BOX))
    col = pos - row * BOX
    cell = jnp.floor(col * 0.5)
    side = (col - 2.0 * cell) * 128.0
    row = jnp.where(row < 48.0, row, row - 96.0)
    half = jnp.floor(row * 0.5)
    row = half + (row - 2.0 * half) * 48.0
    third = jnp.floor((cell + 0.5) * (1.0 / 32.0))
    lane_of = side + jnp.where(row < 72.0, cell, 96.0 + cell - 32.0 * third)
    row = jnp.transpose(jnp.where(row < 72.0, row, row - 72.0 + 24.0 * third))
    lane = lax.broadcasted_iota(jnp.int32, (DEVICES, 256), 1).astype(f32)
    index = lax.broadcasted_iota(jnp.int32, (2 * ROWS, 128), 0)
    index = jnp.where(index < ROWS, index, index - ROWS).astype(f32)
    for slot in range(SLOTS_DEV):
        hit = lane_of[:, slot : slot + 1] == lane
        pack_ref[slot * 128 : (slot + 1) * 128, :] = jnp.where(hit, 1.0, 0.0).astype(bf16)
        hit = jnp.broadcast_to(row[slot : slot + 1, :], (2 * ROWS, 128)) == index
        start = MASK + slot // 2 * 2 * ROWS
        lanes = slice(slot % 2 * 128, slot % 2 * 128 + 128)
        pack_ref[start : start + 2 * ROWS, lanes] = jnp.where(hit, 1.0, 0.0).astype(bf16)


def unfold(block):
    lane = lax.broadcasted_iota(jnp.int32, (24, 128), 1)
    last = pltpu.roll(block[48:72], 96, 1)
    last = jnp.where(lane < 64, pltpu.roll(block[24:48], 64, 1), last)
    last = jnp.where(lane < 32, pltpu.roll(block[:24], 32, 1), last)
    return jnp.concatenate([block, last], axis=0)


def fold(block):
    lane = lax.broadcasted_iota(jnp.int32, (24, 128), 1)
    thirds = [
        jnp.where(lane < 96, block[i * 24 : i * 24 + 24], pltpu.roll(block[72:96], 96 - 32 * i, 1))
        for i in range(3)
    ]
    return jnp.concatenate(thirds, axis=0)


CHUNK = 12


def box_kernel(
    in_ref, pot_any, pack_ref, out_ref, flat, high_v, low_v, grid, mid_h, mid_l, back, picked, pot_ref, sem
):
    move = pltpu.make_async_copy(pot_any, pot_ref, sem)
    move.start()

    def y_table(odd, part):
        start = TABLES + (odd * 2 + part) * 256
        return pack_ref[start : start + 256, :]

    def from_x(odd, rows):
        start = TABLES + 1792 + odd * 192
        return pack_ref[start : start + rows, :BOX]

    for k in range(3):
        flat[k * 128 : (k + 1) * 128, :] = jnp.transpose(in_ref[pl.ds(k, 128, stride=4), :])
    for slot in range(SLOTS_DEV):
        lanes = slice(slot * 128, (slot + 1) * 128)
        values = flat[pl.ds(slot, 24, stride=16), :]
        high = values.astype(bf16).astype(f32)
        high_v[:, lanes] = high
        low_v[:, lanes] = values - high

    def scatter(chunk, carry):
        mask = jnp.concatenate(
            [pack_ref[MASK + i * 2 * ROWS : MASK + (i + 1) * 2 * ROWS, :] for i in range(8)], axis=1
        )
        start = pl.multiple_of(chunk * (CHUNK * 96), 16)
        for part, source in enumerate((high_v, low_v)):
            blocks = []
            for i in range(0, CHUNK, 2):
                first = jnp.broadcast_to(source[pl.ds(chunk * CHUNK + i, 1), :], (8, 2048))
                second = jnp.broadcast_to(source[pl.ds(chunk * CHUNK + i + 1, 1), :], (8, 2048))
                upper = jnp.concatenate([first, first], axis=0).astype(bf16)
                middle = jnp.concatenate([first, second], axis=0).astype(bf16)
                lower = jnp.concatenate([second, second], axis=0).astype(bf16)
                blocks.append(mask * jnp.concatenate([upper] * 4 + [middle] + [lower] * 4, axis=0))
            term = dot(jnp.concatenate(blocks, axis=0), pack_ref[0:MASK, :])
            for odd in range(2):
                for i in range(CHUNK):
                    block = unfold(term[i * ROWS : (i + 1) * ROWS, odd * 128 : odd * 128 + 128])
                    grid[part, odd, pl.ds(start + i * 96, 96), :] = block.astype(bf16)
        return carry

    lax.fori_loop(0, 24 // CHUNK, scatter, 0)

    for part in range(3):
        outs = []
        for odd in range(2):
            high, low = [
                jnp.concatenate(
                    [grid[i, odd, base + part * 384 : base + part * 384 + 384, :] for base in (0, 1152)], axis=1
                )
                for i in range(2)
            ]
            outs.append(dot(high, y_table(odd, 0)) + dot(low, y_table(odd, 0)) + dot(high, y_table(odd, 1)))
        plus, minus = outs[0] + outs[1], outs[0] - outs[1]
        for q in range(2):
            lanes = slice(q * 128, q * 128 + 128)
            high, low = split(jnp.concatenate([plus[:, lanes], minus[:, lanes]], axis=1))
            for i in range(4):
                for half in range(2):
                    block = (slice(i * 96, i * 96 + 96), slice(half * 128, half * 128 + 128))
                    mid_h[part * 4 + i, half, q * 96 : q * 96 + 96, :] = high[block]
                    mid_l[part * 4 + i, half, q * 96 : q * 96 + 96, :] = low[block]

    move.wait()

    def one_plane(i, weight):
        high = jnp.concatenate([mid_h[i, 0], mid_h[i, 1]], axis=1)
        low = jnp.concatenate([mid_l[i, 0], mid_l[i, 1]], axis=1)
        big, small = pack_ref[TABLES + 1024 : TABLES + 1408, :BOX], pack_ref[TABLES + 1408 : TABLES + 1792, :BOX]
        field = dot(big, high) + dot(small, high) + dot(big, low)
        re, im = field[:192] * weight, field[192:] * weight
        for odd in range(2):
            if odd:
                folded = jnp.concatenate([re[:96] - re[96:], im[:96] - im[96:]], axis=0)
            else:
                folded = jnp.concatenate([re[:96] + re[96:], im[:96] + im[96:]], axis=0)
            high, low = split(folded)
            table = from_x(odd, 192)
            out = dot(table[:96], high) + dot(table[96:], high) + dot(table[:96], low)
            start = pl.multiple_of(i * 96 + odd * 48, 8)
            back[pl.ds(start, 48), :] = out[:48]
            back[pl.ds(start + 1152, 48), :] = out[48:]

    def plane(p, carry):
        value = pot_ref[p]
        gap = jnp.zeros((BOX, 32), f32)
        weight = jnp.concatenate([value[:, :HALF], gap, value[:, HALF:], gap], axis=1)
        for i in range(2):
            one_plane(2 * p + i, weight)
        return carry

    lax.fori_loop(0, PLANES, plane, 0, unroll=3)

    for part in range(4):
        re = back[part * 288 : part * 288 + 288, :]
        im = back[1152 + part * 288 : 1152 + part * 288 + 288, :]
        outs = []
        for odd in range(2):
            if odd:
                pair = [re[:, :128] - re[:, 128:], im[:, :128] - im[:, 128:]]
            else:
                pair = [re[:, :128] + re[:, 128:], im[:, :128] + im[:, 128:]]
            high, low = split(jnp.concatenate(pair, axis=1))
            outs.append(
                dot_nt(high, y_table(odd, 0)) + dot_nt(low, y_table(odd, 0)) + dot_nt(high, y_table(odd, 1))
            )
        for q in range(2):
            lanes = slice(q * 128, q * 128 + 128)
            start = q * 12 * ROWS + part * 3 * ROWS
            for odd in range(2):
                rows = [fold(outs[odd][i * 96 : i * 96 + 96, lanes]) for i in range(3)]
                high, low = split(jnp.concatenate(rows, axis=0))
                picked[odd, start : start + 3 * ROWS, :] = high
                picked[2 + odd, start : start + 3 * ROWS, :] = low

    def pick(tile, carry):
        start = pl.multiple_of(tile * 256, 256)
        sel = pack_ref[pl.ds(start, 256), :]
        mask = pack_ref[pl.ds(pl.multiple_of(MASK + tile * 2 * ROWS, 16), 2 * ROWS), :].astype(f32)[:ROWS]
        size = 12 * ROWS
        totals = []
        for i in range(4):
            part = i // 2 * 2
            rows = slice(i % 2 * size, i % 2 * size + size)
            out = dot_nt(jnp.concatenate([picked[part, rows], picked[part + 1, rows]], axis=1), sel)
            totals.append(jnp.sum(out.reshape(12, ROWS, 256) * mask[None], axis=1))
        total = jnp.concatenate([totals[0] + totals[2], totals[1] + totals[3]], axis=0)
        flat[pl.ds(2 * tile, 24, stride=16), :] = total[:, :128]
        flat[pl.ds(2 * tile + 1, 24, stride=16), :] = total[:, 128:]
        return carry

    lax.fori_loop(0, 8, pick, 0, unroll=4)

    for k in range(3):
        out_ref[pl.ds(k, 128, stride=4), :] = jnp.transpose(flat[k * 128 : (k + 1) * 128, :])
    total = jnp.sum(in_ref[pl.ds(3, 128, stride=4), :], axis=0, keepdims=True)
    out_ref[pl.ds(3, 128, stride=4), :] = jnp.broadcast_to(total, (DEVICES, 128))


def apply_kernel(
    count_ref, pos_ref, in_ref, nb_ref, res_ref, z_ref, applied_ref, keep_ref, give_ref, inter_ref,
    halves_ref,
):
    device = lax.axis_index("band") * COLUMNS + lax.axis_index("fft")
    lane = lax.broadcasted_iota(jnp.int32, (COLUMNS, 128), 1) // 32
    pieces = []
    for k in range(3):
        for c in range(4):
            total = jnp.zeros((COLUMNS, 128), f32)
            for group in range(GROUPS):
                piece = in_ref[pl.ds(group * 128 + k, 32, stride=4), :]
                shift = (group - c) * 32 % 128
                if shift:
                    piece = pltpu.roll(piece, shift, 1)
                total = jnp.where(lane == group, piece, total)
            pieces.append(total)
    field = jnp.transpose(jnp.concatenate(pieces, axis=0))
    high, low = split(field)
    parts = live_parts(count_ref[0], nb_ref)
    row = lax.broadcasted_iota(jnp.int32, (NEW * SLOTS_DEV, BOX), 0) & (SLOTS_DEV - 1)
    squares = jnp.zeros((NEW * SLOTS_DEV, BOX), f32)
    for slot in range(SLOTS_DEV):
        pos = pos_ref[device * SLOTS_DEV + slot]
        kx = lax.div(pos, jnp.int32(BOX))
        ky = pos - kx * BOX
        kx = jnp.where(kx < HALF, kx, kx - BOX)
        ky = jnp.where(ky < HALF, ky, ky - BOX)
        squares = jnp.where(row == slot, (kx * kx + ky * ky).astype(f32), squares)
    kz = lax.broadcasted_iota(jnp.int32, (NEW * SLOTS_DEV, BOX), 1)
    kz = jnp.where(kz < HALF, kz, kz - BOX).astype(f32)
    kinetic = 2.0 * (squares + kz * kz) / float(BOX * BOX)
    live = row < count_ref[0]
    applied = []
    for q in range(2):
        table = z_ref[q]
        spectrum = dot(high, table[:384]) + dot(low, table[:384]) + dot(high, table[384:])
        spectrum = spectrum * (1.0 / BOX**3)
        value = jnp.where(live, kinetic * parts[q].astype(f32) + spectrum, 0.0).astype(bf16)
        applied.append(value)
        applied_ref[q] = value.reshape(NEW, SLOTS_DEV, BOX)
    sums = stick_sums(res_ref, applied, halves_ref)
    first = lax.rem(device, 2) == 0
    keep_ref[...] = jnp.where(first, sums[:8], sums[8:])
    give_ref[...] = jnp.where(first, sums[8:], sums[:8])
    inter_ref[...] = in_ref[pl.ds(3, 16, stride=4), :].reshape(2, NEW, RES)


def pair_kernel(keep_ref, came_ref, out_ref):
    total = keep_ref[...] + came_ref[...]
    out_ref[...] = jnp.broadcast_to(total[None], (DEVICES // 2, 8, 128)).reshape(512, 128)


def sum_kernel(in_ref, out_ref):
    total = in_ref[0:8, :]
    for i in range(8, 512, 8):
        total = total + in_ref[i : i + 8, :]
    out_ref[...] = total


def join_kernel(mine_ref, other_ref, out_ref):
    first = lax.rem(lax.axis_index("fft"), 2) == 0
    mine, other = mine_ref[...], other_ref[...]
    low = jnp.where(first, mine, other)
    high = jnp.where(first, other, mine)
    for q in range(2):
        rows = slice(q * 4, q * 4 + 4)
        out_ref[q] = jnp.concatenate([low[rows], high[rows]], axis=0)


WHOLE = 60000 * 1024
vmem = pl.BlockSpec(memory_space=pltpu.VMEM)
smem = pl.BlockSpec(memory_space=pltpu.SMEM)


def call(body, out_shape, in_specs, name, scratch=(), limit=24 << 20):
    return pl.pallas_call(
        body,
        out_shape=out_shape,
        in_specs=in_specs,
        out_specs=jax.tree.map(lambda _: vmem, out_shape),
        scratch_shapes=list(scratch),
        name=name,
        compiler_params=pltpu.CompilerParams(vmem_limit_bytes=limit),
        cost_estimate=pl.CostEstimate(flops=0, bytes_accessed=1 << 20, transcendentals=0),
    )


def shaped(shape, dtype=f32):
    return jax.ShapeDtypeStruct(shape, dtype)


def exchange(values, rows):
    values = values.reshape(DEVICES, rows, 128)
    return lax.all_to_all(values, both, split_axis=0, concat_axis=0, tiled=True)


def local(tables, new_bands, resident, potential, stick_pos, stick_count):
    z_table, box_tables = [jnp.asarray(table) for table in tables]
    resident = jnp.transpose(resident, (0, 2, 3, 1))
    halves_shape = pltpu.VMEM((2, 2, 128, 128), f32)
    sent = call(
        send_kernel, shaped((512, 128)), [smem, vmem, vmem, vmem], "send", scratch=[halves_shape], limit=WHOLE
    )(stick_count, new_bands, resident, z_table)
    came = exchange(sent, 4).reshape(512, 128)
    pack = call(
        place_kernel,
        shaped((TABLES + 2176, 256), bf16),
        [vmem] * 2,
        "place",
        limit=16 << 20,
    )(stick_pos.reshape(DEVICES, SLOTS_DEV), box_tables)
    result = call(
        box_kernel,
        shaped((512, 128)),
        [vmem, pl.BlockSpec(memory_space=pltpu.HBM), vmem],
        "box",
        scratch=[
            pltpu.VMEM((384, 128), f32),
            pltpu.VMEM((24, 2048), f32),
            pltpu.VMEM((24, 2048), f32),
            pltpu.VMEM((2, 2, 2304, 128), bf16),
            pltpu.VMEM((12, 2, 192, 128), bf16),
            pltpu.VMEM((12, 2, 192, 128), bf16),
            pltpu.VMEM((2304, 256), f32),
            pltpu.VMEM((4, 24 * ROWS, 128), bf16),
            pltpu.VMEM((PLANES, BOX, BOX), f32),
            pltpu.SemaphoreType.DMA,
        ],
        limit=40 << 20,
    )(came, pltpu.with_memory_space_constraint(potential, pltpu.HBM), pack)
    returned = exchange(result, 4).reshape(512, 128)
    applied, keep, give, inter = call(
        apply_kernel,
        (
            shaped((2, NEW, SLOTS_DEV, BOX), bf16),
            shaped((8, 128)),
            shaped((8, 128)),
            shaped((2, NEW, RES)),
        ),
        [smem, smem, vmem, vmem, vmem, vmem],
        "apply",
        scratch=[halves_shape],
    )(stick_count, stick_pos, returned, new_bands, resident, z_table)
    pairs = [(i, i ^ 1) for i in range(COLUMNS)]
    other = lax.ppermute(give, "fft", pairs)
    partial = call(pair_kernel, shaped((512, 128)), [vmem, vmem], "pair")(keep, other)
    mine = call(sum_kernel, shaped((8, 128)), [vmem], "total")(exchange(partial, 4).reshape(512, 128))
    other = lax.ppermute(mine, "fft", pairs)
    proj = call(join_kernel, shaped((2, NEW, RES)), [vmem, vmem], "join")(mine, other)
    return applied, jnp.transpose(proj, (0, 2, 1)), jnp.transpose(inter, (0, 2, 1))


def solution(mesh):
    return jax.shard_map(
        functools.partial(local, make_tables()),
        mesh=mesh,
        in_specs=(
            P(None, None, both, None),
            P(None, None, both, None),
            P("fft", None, None),
            P(),
            P(both),
        ),
        out_specs=(P(None, None, both, None), P(), P()),
        check_vma=False,
    )
```
